512 devices in a mesh: dp: 8 (over y, x_hi), seq: 64 (over x_lo, z, core).
Axes of the slice: x: 4 (x_hi: 2, x_lo: 2; x = x_hi * 2 + x_lo), y: 4, z: 16, core: 2. Of those that a mesh axis runs over, the one named last changes fastest.
Arguments:
- signal: bfloat16 [8, 16, 512, 512], P(None, 'dp', 'seq'), may hold values from -6 to 6
- cotangent: bfloat16 [8, 16, 512, 512], P(None, 'dp', 'seq'), may hold values from -6 to 6
- filter_spec: bfloat16 [2, 8, 512, 512], P(None, None, 'seq'), may hold values from -4.1875 to 4.1875
Outputs:
- output: bfloat16 [8, 16, 512, 512], P(None, 'dp', 'seq')
- grad_signal: bfloat16 [8, 16, 512, 512], P(None, 'dp', 'seq')
- grad_filter: bfloat16 [2, 8, 512, 512], P(None, None, 'seq')
The draws below stay inside these ranges and needn't reach their ends.
All inputs are finite; a program needn't handle non-finite values.
Results may differ from the reference program's by a relative error of at most 0.0091.
Values may be sent and summed in bfloat16 or wider, within the bound.
No kernel may reach another device: no remote copies, remote signals or barrier semaphores. Data moves between devices by JAX's collectives and lax.ppermute only.
A program may use at most 64 MiB of HBM per device.

```python
import math
import jax
import jax.numpy as jnp
from jax import lax

NB = 512
NR = 512
FILT = 8
GSIZE = 16


def shard_levels(rng, shape, pieces, smallest, high):
    level = 1.0
    for dim, shards_of in pieces:
        heights = jax.random.uniform(jax.random.fold_in(jax.random.fold_in(rng, 6), dim), (shards_of,), jnp.float32, smallest / len(pieces), high / len(pieces))
        level = level * jnp.repeat(jnp.exp(heights), shape[dim] // shards_of).reshape((-1,) + (1,) * (len(shape) - 1 - dim))
    return level


def centred(rng, dims, spread, reach, cuts=(), kind=jnp.bfloat16):
    entries = jax.random.normal(rng, dims, jnp.float32) * spread
    if len(cuts) > 0:
        entries = shard_levels(rng, dims, cuts, -0.22, 0.18) * entries
    return jnp.clip(entries, min=-reach, max=reach).astype(kind)


def setup_inputs(seed: int = 0) -> dict:
    arg_keys = jax.random.split(jax.random.key(seed), 4)
    signal = centred(arg_keys[0], (FILT, GSIZE, NR, NB), 1.0, 6.0, ((1, 8), (2, 64)))
    cotangent = centred(arg_keys[1], (FILT, GSIZE, NR, NB), 1.0, 6.0, ((1, 8), (2, 64)))
    filter_spec = centred(arg_keys[2], (2, FILT, NB, NR), 0.7, 4.1875, ((2, 64),))
    return {"signal": signal, "cotangent": cotangent, "filter_spec": filter_spec}


def unit_tables(block_size):
    steps_index = jnp.arange(block_size, dtype=jnp.int32)
    product_index = steps_index[:, None] * steps_index[None, :] % block_size
    phases = product_index.astype(jnp.float32) * (2.0 * math.pi / block_size)
    factor = 1.0 / math.sqrt(block_size)
    return ((jnp.cos(phases) * factor).astype(jnp.bfloat16), (-jnp.sin(phases) * factor).astype(jnp.bfloat16))

def twiddle(row_index, col_index, length_all, orient):
    phases = (row_index[:, None] * col_index[None, :]).astype(jnp.float32) * (orient * 2.0 * math.pi / length_all)
    return (jnp.cos(phases), jnp.sin(phases))

def rounded(values):
    return lax.optimization_barrier(values.astype(jnp.bfloat16)).astype(jnp.float32)

def contract(first_operand, second_operand, pattern):
    return jnp.einsum(pattern, first_operand, second_operand, precision=lax.Precision.HIGHEST)

def spectrum(signal_one, big_cos, big_sin, small_cos, small_sin, turn_cos, turn_sin):
    signal_wide = signal_one.astype(jnp.float32)
    real_part = contract(signal_wide, big_cos, 'crs,as->cra')
    imaginary = contract(signal_wide, big_sin, 'crs,as->cra')
    mid_real = rounded(real_part * turn_cos - imaginary * turn_sin)
    mid_imaginary = rounded(real_part * turn_sin + imaginary * turn_cos)
    out_real = contract(mid_real, small_cos, 'cra,qr->caq') - contract(mid_imaginary, small_sin, 'cra,qr->caq')
    out_imaginary = contract(mid_imaginary, small_cos, 'cra,qr->caq') + contract(mid_real, small_sin, 'cra,qr->caq')
    return (out_real, out_imaginary)

def restore(spec_real, spec_imaginary, big_cos, big_sin, small_cos, small_sin, turn_cos, turn_sin):
    real_part = contract(spec_real, small_cos, 'caq,rq->car') + contract(spec_imaginary, small_sin, 'caq,rq->car')
    imaginary = contract(spec_imaginary, small_cos, 'caq,rq->car') - contract(spec_real, small_sin, 'caq,rq->car')
    mid_real = rounded(real_part * turn_cos - imaginary * turn_sin)
    mid_imaginary = rounded(real_part * turn_sin + imaginary * turn_cos)
    total = contract(mid_real, big_cos, 'car,sa->crs') + contract(mid_imaginary, big_sin, 'car,sa->crs')
    return total.astype(jnp.bfloat16)

def reference(signal, cotangent, filter_spec):
    big_table_cos, big_table_sin = unit_tables(NB)
    small_table_cos, small_table_sin = unit_tables(NR)
    big_cos = big_table_cos.astype(jnp.float32)
    big_sin = big_table_sin.astype(jnp.float32)
    small_cos = small_table_cos.astype(jnp.float32)
    small_sin = small_table_sin.astype(jnp.float32)
    freq_index = jnp.arange(NB, dtype=jnp.int32)
    row_index = jnp.arange(NR, dtype=jnp.int32)
    fwd_cos, fwd_sin = twiddle(row_index, freq_index, NB * NR, -1.0)
    inv_cos, inv_sin = twiddle(freq_index, row_index, NB * NR, 1.0)
    filter_reals = filter_spec[0].astype(jnp.float32)
    filter_imags = filter_spec[1].astype(jnp.float32)

    def group_step(carried, inputs):
        signal_one, cotangent_one, filter_real, filter_imaginary = inputs
        sig_real, sig_imaginary = spectrum(signal_one, big_cos, big_sin, small_cos, small_sin, fwd_cos, fwd_sin)
        cot_real, cot_imaginary = spectrum(cotangent_one, big_cos, big_sin, small_cos, small_sin, fwd_cos, fwd_sin)
        filter_real = filter_real[None]
        filter_imaginary = filter_imaginary[None]
        prod_real = rounded(filter_real * sig_real - filter_imaginary * sig_imaginary)
        prod_imaginary = rounded(filter_real * sig_imaginary + filter_imaginary * sig_real)
        back_real = rounded(filter_real * cot_real + filter_imaginary * cot_imaginary)
        back_imaginary = rounded(filter_real * cot_imaginary - filter_imaginary * cot_real)
        output_one = restore(prod_real, prod_imaginary, big_cos, big_sin, small_cos, small_sin, inv_cos, inv_sin)
        grad_one = restore(back_real, back_imaginary, big_cos, big_sin, small_cos, small_sin, inv_cos, inv_sin)
        grad_terms = jnp.stack([lax.optimization_barrier(jnp.sum(cot_real * sig_real + cot_imaginary * sig_imaginary, axis=0)), lax.optimization_barrier(jnp.sum(cot_imaginary * sig_real - cot_real * sig_imaginary, axis=0))])
        return (carried, (output_one, grad_one, grad_terms.astype(jnp.bfloat16)))
    initial = jnp.zeros((), jnp.float32)
    unused, (output, grad_signal, grad_groups) = lax.scan(group_step, initial, (signal, cotangent, filter_reals, filter_imags))
    grad_filter = jnp.transpose(grad_groups, (1, 0, 2, 3))
    return (output, grad_signal, grad_filter)
```

```python
import math

import jax
import jax.numpy as jnp
import numpy as np
from jax import lax
from jax.experimental import pallas as pl
from jax.experimental.pallas import tpu as pltpu
from jax.sharding import PartitionSpec as P

N = 512
SEQ = 64
ROWS = N // SEQ
BF = jnp.bfloat16
F32 = jnp.float32
VMEM = pl.BlockSpec(memory_space=pltpu.VMEM)
SMEM = pl.BlockSpec(memory_space=pltpu.SMEM)


def unit_tables():
    steps = np.arange(N, dtype=np.int32)
    phases = (steps[:, None] * steps[None, :] % N).astype(np.float32) * np.float32(
        2.0 * math.pi / N
    )
    factor = np.float32(1.0 / math.sqrt(N))
    return (np.cos(phases) * factor).astype(BF), (-np.sin(phases) * factor).astype(BF)


def row_order():
    lane = np.arange(N)
    return 8 * (lane % 64) + 2 * (lane // 128) + (lane // 64) % 2


def first_table():
    cos_t, sin_t = unit_tables()
    order = row_order()
    return np.concatenate([cos_t[:, order], sin_t[:, order]], axis=1)


def selectors():
    lane = np.arange(256)
    row = 2 * (lane // 32 % 4) + lane // 128
    kind = lane // 16 % 2
    filt = lane // 2 % 8
    hit = (filt * 8 + row)[None, :] == np.arange(64)[:, None]
    expand = hit.astype(np.float32)
    signed = expand * np.where(kind == 1, -1.0, 1.0)[None, :]
    gather = expand * (kind == 0)[None, :]
    return (
        np.concatenate([expand, signed], axis=1).astype(BF),
        gather.astype(np.float32),
    )


def dot(a, b, dims=((1,), (0,)), precision=None):
    return lax.dot_general(a, b, (dims, ((), ())), precision=precision, preferred_element_type=F32)


def turn(idx_ref):
    shape = (ROWS, N)
    lane = lax.broadcasted_iota(jnp.int32, shape, 1)
    row = idx_ref[0] * ROWS + lax.broadcasted_iota(jnp.int32, shape, 0)
    col = 8 * (lane & 63) + 2 * (lane >> 7) + ((lane >> 6) & 1)
    phases = (row * col).astype(F32) * (-2.0 * math.pi / (N * N))
    return jnp.cos(phases), jnp.sin(phases)


def kernel_a(idx_ref, sig_ref, cot_ref, t_ref, out_ref, yre, yim, z):
    tc, ts = turn(idx_ref)
    for half, ref in enumerate((sig_ref, cot_ref)):
        x = ref[...]
        re = dot(x, t_ref[:, :N]).reshape(16, ROWS, N)
        im = dot(x, t_ref[:, N:]).reshape(16, ROWS, N)
        at = pl.ds(half * 128, 128)
        for y, v in ((yre, re * tc - im * ts), (yim, re * ts + im * tc)):
            v = v.reshape(128, N)
            for s in range(4):
                y[s, at, :] = v[:, s * 128 : (s + 1) * 128]
    for r in range(ROWS):
        for ri, y in enumerate((yre, yim)):
            rows = [y[s, pl.ds(r, 32, stride=ROWS), :] for s in range(4)]
            block = jnp.concatenate(rows, axis=0).T
            for p in range(2):
                z[ri * 2 + p, pl.ds(r, 64, stride=ROWS), :] = block[p * 64 : (p + 1) * 64]
    for k in range(4):
        out_ref[:, k * 128 : (k + 1) * 128] = z[k].astype(BF)


def kernel_f(f_ref, sel_ref, h_ref):
    for ri in range(2):
        cols = pl.ds(ri * 256, 256)
        h_ref[:, cols] = dot(f_ref[ri], sel_ref[:, cols], ((0,), (0,))).astype(BF)


def kernel_b(r_ref, wc_ref, ws_ref, h_ref, gather_ref, v_ref, g_ref, prod):
    for k in range(4):
        at = pl.ds(k * 128, 128)
        p1 = dot(wc_ref[at, :], r_ref[...])
        p2 = dot(ws_ref[at, :], r_ref[...])
        xre = p1[:, :256] - p2[:, 256:]
        xim = p1[:, 256:] + p2[:, :256]
        hre = h_ref[at, :256].astype(F32)
        him = h_ref[at, 256:].astype(F32)
        prod[at, :256] = (hre * xre - him * xim).astype(BF)
        prod[at, 256:] = (hre * xim + him * xre).astype(BF)
        cre = pltpu.roll(xre, 240, 1)
        cim = pltpu.roll(xim, 240, 1)
        for ri, g in enumerate((cre * xre + cim * xim, cim * xre - cre * xim)):
            g_ref[ri, :, at] = dot(
                gather_ref[...], g, ((1,), (1,)), lax.Precision.HIGHEST
            ).astype(BF)
    for k in range(4):
        at = pl.ds(k * 128, 128)
        q1 = dot(wc_ref[at, :], prod[...])
        q2 = dot(ws_ref[at, :], prod[...])
        v_ref[at, :256] = (q1[:, :256] + q2[:, 256:]).astype(BF)
        v_ref[at, 256:] = (q1[:, 256:] - q2[:, :256]).astype(BF)


def kernel_c(idx_ref, v_ref, t_ref, out_ref, grad_ref, z, yre, yim):
    for k in range(4):
        z[k] = v_ref[:, k * 128 : (k + 1) * 128].astype(F32)
    for r in range(ROWS):
        for ri, y in enumerate((yre, yim)):
            rows = [z[ri * 2 + p, pl.ds(r, 64, stride=ROWS), :] for p in range(2)]
            block = jnp.concatenate(rows, axis=0).T
            for s in range(4):
                y[s, pl.ds(r, 32, stride=ROWS), :] = block[s * 32 : (s + 1) * 32]
    tc, ts = turn(idx_ref)
    for half, ref in enumerate((out_ref, grad_ref)):
        at = pl.ds(half * 128, 128)
        re, im = (
            jnp.concatenate([y[s, at, :] for s in range(4)], axis=1).reshape(16, ROWS, N)
            for y in (yre, yim)
        )
        mid_re = (re * tc + im * ts).reshape(128, N).astype(BF)
        mid_im = (im * tc - re * ts).reshape(128, N).astype(BF)
        total = dot(mid_re, t_ref[:, :N], ((1,), (1,))) + dot(mid_im, t_ref[:, N:], ((1,), (1,)))
        ref[...] = total.astype(BF)


def body(signal, cotangent, filter_spec):
    shape = signal.shape
    place = lax.axis_index("seq").astype(jnp.int32).reshape(1)
    table = jnp.asarray(first_table())
    cos_t, sin_t = (jnp.asarray(t) for t in unit_tables())
    expand, gather = (jnp.asarray(t) for t in selectors())
    with jax.named_scope("kernel_a"):
        sent = pl.pallas_call(
            kernel_a,
            in_specs=[SMEM, VMEM, VMEM, VMEM],
            out_specs=VMEM,
            out_shape=jax.ShapeDtypeStruct((N, N), BF),
            scratch_shapes=[
                pltpu.VMEM((4, 256, 128), F32),
                pltpu.VMEM((4, 256, 128), F32),
                pltpu.VMEM((4, N, 128), F32),
            ],
        )(place, signal.reshape(128, N), cotangent.reshape(128, N), table)
    with jax.named_scope("first_exchange"):
        got = lax.all_to_all(sent.reshape(SEQ, ROWS, N), "seq", 0, 0, tiled=True).reshape(N, N)
    with jax.named_scope("kernel_f"):
        spread = pl.pallas_call(
            kernel_f,
            in_specs=[VMEM, VMEM],
            out_specs=VMEM,
            out_shape=jax.ShapeDtypeStruct((N, N), BF),
            cost_estimate=pl.CostEstimate(flops=67108864, bytes_accessed=720896, transcendentals=0),
        )(filter_spec.reshape(2, 64, N), expand)
    with jax.named_scope("kernel_b"):
        back, grad = pl.pallas_call(
            kernel_b,
            in_specs=[VMEM] * 5,
            out_specs=[VMEM, VMEM],
            out_shape=[
                jax.ShapeDtypeStruct((N, N), BF),
                jax.ShapeDtypeStruct((2, 64, N), BF),
            ],
            scratch_shapes=[pltpu.VMEM((N, N), BF)],
        )(got, cos_t, sin_t, spread, gather)
    with jax.named_scope("second_exchange"):
        mid = lax.all_to_all(back.reshape(SEQ, ROWS, N), "seq", 0, 0, tiled=True).reshape(N, N)
    for bit in (1, 2, 4):
        with jax.named_scope(f"grad_sum_{bit}"):
            other = lax.ppermute(grad, "dp", [(d, d ^ bit) for d in range(8)])
            grad = (grad.astype(F32) + other.astype(F32)).astype(BF)
    with jax.named_scope("kernel_c"):
        output, grad_signal = pl.pallas_call(
            kernel_c,
            in_specs=[SMEM, VMEM, VMEM],
            out_specs=[VMEM, VMEM],
            out_shape=[jax.ShapeDtypeStruct((128, N), BF)] * 2,
            scratch_shapes=[
                pltpu.VMEM((4, N, 128), F32),
                pltpu.VMEM((4, 256, 128), F32),
                pltpu.VMEM((4, 256, 128), F32),
            ],
        )(place, mid, table)
    return output.reshape(shape), grad_signal.reshape(shape), grad.reshape(2, 8, 8, N)


def solution(mesh):
    placed = (P(None, "dp", "seq", None), P(None, "dp", "seq", None), P(None, None, "seq", None))
    return jax.shard_map(
        body, mesh=mesh, in_specs=placed, out_specs=placed, check_vma=False
    )
```

```python
import math

import jax
import jax.numpy as jnp
import numpy as np
from jax import lax
from jax.experimental import pallas as pl
from jax.experimental.pallas import tpu as pltpu
from jax.sharding import PartitionSpec as P

N = 512
SEQ = 64
ROWS = N // SEQ
HALF = N // 2
BF = jnp.bfloat16
F32 = jnp.float32
VMEM = pl.BlockSpec(memory_space=pltpu.VMEM)
SMEM = pl.BlockSpec(memory_space=pltpu.SMEM)
PARAMS = pltpu.CompilerParams(vmem_limit_bytes=20 * 2**20)


def unit_tables():
    steps = np.arange(N, dtype=np.int32)
    phases = (steps[:, None] * steps[None, :] % N).astype(np.float32) * np.float32(
        2.0 * math.pi / N
    )
    factor = np.float32(1.0 / math.sqrt(N))
    return (np.cos(phases) * factor).astype(BF), (-np.sin(phases) * factor).astype(BF)


def first_table():
    cos_t, sin_t = unit_tables()
    col = np.arange(HALF)
    place = col % 64
    row = 8 * place + 2 * (col // 128) + col // 64 % 2 + (place >= 32)
    re, im = cos_t[:, row], sin_t[:, row]
    im[:, 0] = cos_t[:, HALF]
    return np.concatenate([re, im], axis=1)


def lanes():
    lane = np.arange(HALF)
    slot = 2 * (lane // 32 % 2) + lane // 128
    return slot, lane // 64 % 2, lane // 16 % 2, lane // 2 % 8, lane % 2


def filter_selectors():
    slot, _, _, filt, chan = lanes()
    own = np.zeros((3, 112, HALF), np.float32)
    mirror = np.zeros((3, 112, HALF), np.float32)
    for lane in range(HALF):
        k, f = slot[lane], filt[lane]
        for kind in (0, 1):
            own[kind, f * 8 + k, lane] = 0.5
            mirror[kind, 96 + f if k == 0 else 64 + f * 4 + 4 - k, lane] = 0.5
        own[2, f * 8 + k + 1, lane] = 0.5
        mirror[2, 64 + f * 4 + 3 - k, lane] = 0.5
        if k == 0:
            own[0, :, lane] = 0
            mirror[0, :, lane] = 0
            source = 96 + f if chan[lane] else f * 8
            own[0, source, lane] = 0.5
            mirror[0, source, lane] = 0.5
    return own.astype(BF), mirror.astype(BF)


def gather_tables():
    slot, part, kind, filt, chan = lanes()
    out = np.zeros((2, 2, 48, HALF), np.float32)
    for lane in range(HALF):
        if kind[lane]:
            continue
        for first in range(2):
            for ri in range(2):
                sign = -1.0 if ri and part[lane] else 1.0
                extra = slot[lane] == 0 and chan[lane] == 1
                if not (first and extra):
                    out[first, ri, slot[lane] * 8 + filt[lane], lane] = sign
                if extra:
                    out[first, ri, 32 + filt[lane], lane] = sign
    return out


def grad_selectors():
    own = np.zeros((4, 64, 112), np.float32)
    mirror = np.zeros((4, 64, 112), np.float32)
    for f in range(8):
        for row in range(8):
            at = f * 8 + row
            for kind in (0, 1):
                if row < 4:
                    own[kind, at, row * 8 + f] = 1
                else:
                    mirror[kind, at, 48 + (7 - row) * 8 + f] = 1
            for kind in (2, 3):
                if row == 0:
                    mirror[kind, at, 96 + f] = 1
                elif row < 5:
                    own[kind, at, (row - 1) * 8 + f] = 1
                else:
                    mirror[kind, at, 48 + (8 - row) * 8 + f] = 1
        own[0, f * 8, f] = 0.5
        mirror[0, f * 8, f] = 0.5
        own[3, f * 8, 96 + f] = 0.5
        mirror[3, f * 8, 96 + f] = 0.5
    return own.astype(BF), mirror.astype(BF)


def payload_selectors():
    tail = np.zeros((32, 64), np.float32)
    head = np.zeros((8, 64), np.float32)
    for f in range(8):
        head[f, f * 8] = 1
        for row in range(4):
            tail[f * 4 + row, f * 8 + 4 + row] = 1
    return tail.astype(BF), head.astype(BF)


def dot(a, b, dims=((1,), (0,)), precision=None):
    return lax.dot_general(a, b, (dims, ((), ())), precision=precision, preferred_element_type=F32)


def turn(idx_ref, chan):
    shape = (ROWS, HALF)
    lane = lax.broadcasted_iota(jnp.int32, shape, 1)
    row = idx_ref[0] * ROWS + lax.broadcasted_iota(jnp.int32, shape, 0)
    place = lane & 63
    col = 8 * place + 2 * (lane >> 7) + ((lane >> 6) & 1) + (place >> 5)
    if chan:
        col = jnp.where(lane == 0, HALF, col)
    phases = (row * col).astype(F32) * (-2.0 * math.pi / (N * N))
    return jnp.cos(phases), jnp.sin(phases)


def swap_first(re, im):
    first = lax.broadcasted_iota(jnp.int32, re[0].shape, 2) == 0
    return (re[0], jnp.where(first, im[0], re[1])), (jnp.where(first, re[1], im[0]), im[1])


def kernel_a(idx_ref, sig_ref, cot_ref, t_ref, f_ref, tail_ref, head_ref, out_ref, tails_ref,
             heads_ref, yre, yim, z):
    for ri in range(2):
        tails_ref[ri] = dot(tail_ref[...], f_ref[ri]).astype(BF)
        heads_ref[ri] = dot(head_ref[...], f_ref[ri]).astype(BF)
    turns = [turn(idx_ref, chan) for chan in range(2)]
    for half, ref in enumerate((sig_ref, cot_ref)):
        x = ref[...]
        re = dot(x, t_ref[:, :HALF]).reshape(8, 2, ROWS, HALF)
        im = dot(x, t_ref[:, HALF:]).reshape(8, 2, ROWS, HALF)
        re, im = swap_first((re[:, 0], re[:, 1]), (im[:, 0], im[:, 1]))
        at = pl.ds(half * 128, 128)
        out_re = [re[c] * turns[c][0] - im[c] * turns[c][1] for c in range(2)]
        out_im = [re[c] * turns[c][1] + im[c] * turns[c][0] for c in range(2)]
        for y, v in ((yre, out_re), (yim, out_im)):
            v = jnp.stack(v, axis=1).reshape(128, HALF)
            for s in range(2):
                y[s, at, :] = v[:, s * 128 : (s + 1) * 128]
    for r in range(ROWS):
        rows = [y[s, pl.ds(r, 32, stride=ROWS), :] for y in (yre, yim) for s in range(2)]
        block = jnp.concatenate(rows, axis=0).T
        for p in range(2):
            z[p, pl.ds(r, 64, stride=ROWS), :] = block[p * 64 : (p + 1) * 64]
    for p in range(2):
        out_ref[:, p * 128 : (p + 1) * 128] = z[p].astype(BF)


def kernel_f(idx_ref, f_ref, tail_ref, head_ref, own_ref, mirror_ref, flip_ref, h_ref, rows):
    place = idx_ref[0]
    kind = jnp.where(place == 0, 0, jnp.where(place < 32, 1, 2))
    rows[:, :64, :] = f_ref[...]
    rows[:, 64:96, :] = tail_ref[...]
    rows[:, 96:, :] = jnp.zeros((2, 16, N), BF)
    rows[:, 96:104, :] = head_ref[...]
    lane = lax.broadcasted_iota(jnp.int32, (N, HALF), 1)
    shifted = ((lane & ~30) == 0) | ((lane & ~30) == 64)
    shifted = shifted & (place == 0)
    negative = ((lane >> 6) & 1) == ((lane >> 4) & 1)
    for ri in range(2):
        near = dot(rows[ri], own_ref[kind], ((0,), (0,)))
        far = dot(rows[ri], mirror_ref[kind], ((0,), (0,))).astype(BF)
        far = dot(flip_ref[...], far)
        far = jnp.where(shifted, pltpu.roll(far, 1, 0), far)
        if ri == 0:
            h_ref[:, :HALF] = near + far
        else:
            value = near - far
            h_ref[:, HALF:] = jnp.where(negative, -value, value)


def kernel_b(idx_ref, r_ref, wc_ref, ws_ref, h_ref, gather_ref, v_ref, g_ref, prod):
    first = jnp.where(idx_ref[0] == 0, 1, 0)
    sign = jnp.where(lax.broadcasted_iota(jnp.int32, (128, 128), 1) < 64, -1.0, 1.0)
    for k in range(4):
        at = pl.ds(k * 128, 128)
        p1 = dot(wc_ref[at, :], r_ref[...])
        p2 = dot(ws_ref[at, :], r_ref[...])
        pairs = []
        for p in range(2):
            cols = slice(p * 128, (p + 1) * 128)
            x = p1[:, cols] + sign * pltpu.roll(p2[:, cols], 64, 1)
            swapped = pltpu.roll(x, 64, 1)
            h1 = h_ref[at, p * 128 : (p + 1) * 128]
            h2 = h_ref[at, HALF + p * 128 : HALF + (p + 1) * 128]
            prod[at, cols] = (h1 * x + h2 * swapped).astype(BF)
            pairs.append((pltpu.roll(x, 112, 1) * x, pltpu.roll(x, 48, 1) * x))
        for ri in range(2):
            terms = jnp.concatenate([pairs[0][ri], pairs[1][ri]], axis=1)
            g_ref[ri, :, at] = dot(
                gather_ref[first, ri], terms, ((1,), (1,)), lax.Precision.HIGHEST
            ).astype(BF)
    for k in range(4):
        at = pl.ds(k * 128, 128)
        q1 = dot(wc_ref[at, :], prod[...])
        q2 = dot(ws_ref[at, :], prod[...])
        for p in range(2):
            cols = slice(p * 128, (p + 1) * 128)
            v_ref[at, cols] = (q1[:, cols] - sign * pltpu.roll(q2[:, cols], 64, 1)).astype(BF)


def kernel_c(idx_ref, v_ref, t_ref, out_ref, grad_ref, z, yre, yim):
    for p in range(2):
        z[p] = v_ref[:, p * 128 : (p + 1) * 128].astype(F32)
    for r in range(ROWS):
        rows = [z[p, pl.ds(r, 64, stride=ROWS), :] for p in range(2)]
        block = jnp.concatenate(rows, axis=0).T
        for ri, y in enumerate((yre, yim)):
            for s in range(2):
                at = ri * 64 + s * 32
                y[s, pl.ds(r, 32, stride=ROWS), :] = block[at : at + 32]
    double = jnp.where(lax.broadcasted_iota(jnp.int32, (ROWS, HALF), 1) == 0, 1.0, 2.0)
    turns = [[t * double for t in turn(idx_ref, chan)] for chan in range(2)]
    for half, ref in enumerate((out_ref, grad_ref)):
        at = pl.ds(half * 128, 128)
        re, im = (
            jnp.concatenate([y[s, at, :] for s in range(2)], axis=1).reshape(8, 2, ROWS, HALF)
            for y in (yre, yim)
        )
        mid_re = [re[:, c] * turns[c][0] + im[:, c] * turns[c][1] for c in range(2)]
        mid_im = [im[:, c] * turns[c][0] - re[:, c] * turns[c][1] for c in range(2)]
        mid_re, mid_im = (
            jnp.stack(v, axis=1).reshape(128, HALF).astype(BF) for v in swap_first(mid_re, mid_im)
        )
        total = dot(mid_re, t_ref[:, :HALF], ((1,), (1,)))
        total = total + dot(mid_im, t_ref[:, HALF:], ((1,), (1,)))
        ref[...] = total.astype(BF)


def kernel_g(idx_ref, g0_ref, g1_ref, far0_ref, far1_ref, head0_ref, head1_ref, own_ref,
             mirror_ref, flip_ref, out_ref, rows):
    place = idx_ref[0]
    kind = jnp.where(
        place == 0, 0, jnp.where(place == 32, 3, jnp.where(place < 32, 1, 2))
    )
    sources = ((g0_ref, far0_ref, head0_ref), (g1_ref, far1_ref, head1_ref))
    for k, (g_ref, far_ref, head_ref) in enumerate(sources):
        rows[k, :, :48, :] = g_ref[...]
        rows[k, :, 48:96, :] = far_ref[...]
        rows[k, :, 96:, :] = jnp.zeros((2, 16, N), BF)
        rows[k, :, 96:104, :] = head_ref[...]
    row = lax.broadcasted_iota(jnp.int32, (64, N), 0)
    shifted = ((row & 7) == 0) & (place == 0)
    for ri in range(2):
        near = dot(own_ref[kind], rows[0, ri]) + dot(own_ref[kind], rows[1, ri])
        far = [
            dot(dot(mirror_ref[kind], rows[k, ri]).astype(BF), flip_ref[...]) for k in range(2)
        ]
        far = far[0] + far[1]
        far = jnp.where(shifted, pltpu.roll(far, 1, 1), far)
        out_ref[ri] = (near + far if ri == 0 else near - far).astype(BF)


def across(moves):
    return [(d * SEQ + a, (d ^ 1) * SEQ + b) for d in range(8) for a, b in moves]


def body(signal, cotangent, filter_spec):
    shape = signal.shape
    place = lax.axis_index("seq").astype(jnp.int32).reshape(1)
    table = jnp.asarray(first_table())
    cos_t, sin_t = (jnp.asarray(t) for t in unit_tables())
    flip = jnp.asarray(np.eye(N, dtype=np.float32)[::-1].astype(BF))
    tail, head = (jnp.asarray(t) for t in payload_selectors())
    f_own, f_mirror = (jnp.asarray(t) for t in filter_selectors())
    g_own, g_mirror = (jnp.asarray(t) for t in grad_selectors())
    gather = jnp.asarray(gather_tables())
    opposite = [(d, SEQ - 1 - d) for d in range(SEQ)]
    heads_to = [(d, {0: 32, 32: 0}.get(d, SEQ - d)) for d in range(SEQ)]
    filt = filter_spec.reshape(2, 64, N)
    with jax.named_scope("kernel_a"):
        sent, tails, heads = pl.pallas_call(
            kernel_a,
            in_specs=[SMEM] + [VMEM] * 6,
            out_specs=[VMEM] * 3,
            out_shape=[
                jax.ShapeDtypeStruct((N, HALF), BF),
                jax.ShapeDtypeStruct((2, 32, N), BF),
                jax.ShapeDtypeStruct((2, 8, N), BF),
            ],
            scratch_shapes=[
                pltpu.VMEM((2, 256, 128), F32),
                pltpu.VMEM((2, 256, 128), F32),
                pltpu.VMEM((2, N, 128), F32),
            ],
        )(place, signal.reshape(128, N), cotangent.reshape(128, N), table, filt, tail, head)
    with jax.named_scope("first_exchange"):
        got = lax.all_to_all(sent.reshape(SEQ, ROWS, HALF), "seq", 0, 0, tiled=True)
    with jax.named_scope("filter_mirror"):
        tails = lax.ppermute(tails, "seq", opposite)
        heads = lax.ppermute(heads, "seq", heads_to)
    with jax.named_scope("kernel_f"):
        spread = pl.pallas_call(
            kernel_f,
            in_specs=[SMEM] + [VMEM] * 6,
            out_specs=VMEM,
            out_shape=jax.ShapeDtypeStruct((N, N), F32),
            scratch_shapes=[pltpu.VMEM((2, 112, N), BF)],
            compiler_params=PARAMS,
            cost_estimate=pl.CostEstimate(
                flops=400000000, bytes_accessed=2000000, transcendentals=0
            ),
        )(place, filt, tails, heads, f_own, f_mirror, flip)
    with jax.named_scope("kernel_b"):
        back, grad = pl.pallas_call(
            kernel_b,
            in_specs=[SMEM] + [VMEM] * 5,
            out_specs=[VMEM, VMEM],
            out_shape=[
                jax.ShapeDtypeStruct((N, HALF), BF),
                jax.ShapeDtypeStruct((2, 48, N), BF),
            ],
            scratch_shapes=[pltpu.VMEM((N, HALF), BF)],
            compiler_params=PARAMS,
        )(place, got.reshape(N, HALF), cos_t, sin_t, spread, gather)
    with jax.named_scope("second_exchange"):
        mid = lax.all_to_all(back.reshape(SEQ, ROWS, HALF), "seq", 0, 0, tiled=True)
    with jax.named_scope("grad_sum"):
        parts = [lax.ppermute(grad, "dp", [(d, d ^ bit) for d in range(8)]) for bit in (2, 4, 6)]
        wide = [v.astype(F32) for v in [grad] + parts]
        grad = ((wide[0] + wide[1]) + (wide[2] + wide[3])).astype(BF)
    with jax.named_scope("grad_mirror"):
        slot = jnp.where(place[0] == 0, grad[:, 32:40], grad[:, :8])
        both = ("dp", "seq")
        far0 = lax.ppermute(grad, "seq", opposite)
        far1 = lax.ppermute(grad, both, across(opposite))
        slot0 = lax.ppermute(slot, "seq", heads_to)
        slot1 = lax.ppermute(slot, both, across(heads_to))
        grad1 = lax.ppermute(grad, "dp", [(d, d ^ 1) for d in range(8)])
    with jax.named_scope("kernel_c"):
        output, grad_signal = pl.pallas_call(
            kernel_c,
            in_specs=[SMEM, VMEM, VMEM],
            out_specs=[VMEM, VMEM],
            out_shape=[jax.ShapeDtypeStruct((128, N), BF)] * 2,
            scratch_shapes=[
                pltpu.VMEM((2, N, 128), F32),
                pltpu.VMEM((2, 256, 128), F32),
                pltpu.VMEM((2, 256, 128), F32),
            ],
            compiler_params=PARAMS,
            cost_estimate=pl.CostEstimate(
                flops=400000000, bytes_accessed=2000000, transcendentals=0
            ),
        )(place, mid.reshape(N, HALF), table)
    with jax.named_scope("kernel_g"):
        grad_filter = pl.pallas_call(
            kernel_g,
            in_specs=[SMEM] + [VMEM] * 9,
            out_specs=VMEM,
            out_shape=jax.ShapeDtypeStruct((2, 64, N), BF),
            scratch_shapes=[pltpu.VMEM((2, 2, 112, N), BF)],
            compiler_params=PARAMS,
            cost_estimate=pl.CostEstimate(
                flops=100000000, bytes_accessed=1000000, transcendentals=0
            ),
        )(place, grad, grad1, far0, far1, slot0, slot1, g_own, g_mirror, flip)
    return output.reshape(shape), grad_signal.reshape(shape), grad_filter.reshape(2, 8, 8, N)


def solution(mesh):
    placed = (P(None, "dp", "seq", None), P(None, "dp", "seq", None), P(None, None, "seq", None))
    return jax.shard_map(
        body, mesh=mesh, in_specs=placed, out_specs=placed, check_vma=False
    )
```

```python
import math

import jax
import jax.numpy as jnp
import numpy as np
from jax import lax
from jax.experimental import pallas as pl
from jax.experimental.pallas import tpu as pltpu
from jax.sharding import PartitionSpec as P

N = 512
SEQ = 64
ROWS = N // SEQ
HALF = N // 2
BF = jnp.bfloat16
F32 = jnp.float32
VMEM = pl.BlockSpec(memory_space=pltpu.VMEM)
SMEM = pl.BlockSpec(memory_space=pltpu.SMEM)
PARAMS = pltpu.CompilerParams(vmem_limit_bytes=20 * 2**20)


def unit_tables():
    steps = np.arange(N, dtype=np.int32)
    phases = (steps[:, None] * steps[None, :] % N).astype(np.float32) * np.float32(
        2.0 * math.pi / N
    )
    factor = np.float32(1.0 / math.sqrt(N))
    return (np.cos(phases) * factor).astype(BF), (-np.sin(phases) * factor).astype(BF)


def first_table():
    cos_t, sin_t = unit_tables()
    col = np.arange(HALF)
    place = col % 64
    row = 8 * place + 2 * (col // 128) + col // 64 % 2 + (place >= 32)
    re, im = cos_t[:, row], sin_t[:, row]
    im[:, 0] = cos_t[:, HALF]
    return np.concatenate([re, im], axis=1)


def lanes():
    lane = np.arange(HALF)
    slot = 2 * (lane // 32 % 2) + lane // 128
    return slot, lane // 64 % 2, lane // 16 % 2, lane // 2 % 8, lane % 2


def filter_selectors():
    slot, _, _, filt, chan = lanes()
    own = np.zeros((3, 112, HALF), np.float32)
    mirror = np.zeros((3, 112, HALF), np.float32)
    for lane in range(HALF):
        k, f = slot[lane], filt[lane]
        for kind in (0, 1):
            own[kind, f * 8 + k, lane] = 0.5
            mirror[kind, 96 + f if k == 0 else 64 + f * 4 + 4 - k, lane] = 0.5
        own[2, f * 8 + k + 1, lane] = 0.5
        mirror[2, 64 + f * 4 + 3 - k, lane] = 0.5
        if k == 0:
            own[0, :, lane] = 0
            mirror[0, :, lane] = 0
            source = 96 + f if chan[lane] else f * 8
            own[0, source, lane] = 0.5
            mirror[0, source, lane] = 0.5
    return own.astype(BF), mirror.astype(BF)


def gather_tables():
    slot, part, kind, filt, chan = lanes()
    out = np.zeros((2, 2, 48, HALF), np.float32)
    for lane in range(HALF):
        if kind[lane]:
            continue
        for first in range(2):
            for ri in range(2):
                sign = -1.0 if ri and part[lane] else 1.0
                extra = slot[lane] == 0 and chan[lane] == 1
                if not (first and extra):
                    out[first, ri, slot[lane] * 8 + filt[lane], lane] = sign
                if extra:
                    out[first, ri, 32 + filt[lane], lane] = sign
    return out


def grad_selectors():
    own = np.zeros((4, 64, 112), np.float32)
    mirror = np.zeros((4, 64, 112), np.float32)
    for f in range(8):
        for row in range(8):
            at = f * 8 + row
            for kind in (0, 1):
                if row < 4:
                    own[kind, at, row * 8 + f] = 1
                else:
                    mirror[kind, at, 48 + (7 - row) * 8 + f] = 1
            for kind in (2, 3):
                if row == 0:
                    mirror[kind, at, 96 + f] = 1
                elif row < 5:
                    own[kind, at, (row - 1) * 8 + f] = 1
                else:
                    mirror[kind, at, 48 + (8 - row) * 8 + f] = 1
        own[0, f * 8, f] = 0.5
        mirror[0, f * 8, f] = 0.5
        own[3, f * 8, 96 + f] = 0.5
        mirror[3, f * 8, 96 + f] = 0.5
    return own.astype(BF), mirror.astype(BF)


def payload_selectors():
    tail = np.zeros((32, 64), np.float32)
    head = np.zeros((8, 64), np.float32)
    for f in range(8):
        head[f, f * 8] = 1
        for row in range(4):
            tail[f * 4 + row, f * 8 + 4 + row] = 1
    return tail.astype(BF), head.astype(BF)


def dot(a, b, dims=((1,), (0,)), precision=None):
    return lax.dot_general(a, b, (dims, ((), ())), precision=precision, preferred_element_type=F32)


def turn(idx_ref, chan):
    shape = (ROWS, HALF)
    lane = lax.broadcasted_iota(jnp.int32, shape, 1)
    row = idx_ref[0] * ROWS + lax.broadcasted_iota(jnp.int32, shape, 0)
    place = lane & 63
    col = 8 * place + 2 * (lane >> 7) + ((lane >> 6) & 1) + (place >> 5)
    if chan:
        col = jnp.where(lane == 0, HALF, col)
    phases = (row * col).astype(F32) * (-2.0 * math.pi / (N * N))
    return jnp.cos(phases), jnp.sin(phases)


def swap_first(re, im):
    first = lax.broadcasted_iota(jnp.int32, re[0].shape, 2) == 0
    return (re[0], jnp.where(first, im[0], re[1])), (jnp.where(first, re[1], im[0]), im[1])


def kernel_a(idx_ref, sig_ref, cot_ref, t_ref, f_ref, tail_ref, head_ref, out_ref, tails_ref,
             heads_ref, yre, yim, z):
    for ri in range(2):
        tails_ref[ri] = dot(tail_ref[...], f_ref[ri]).astype(BF)
        heads_ref[ri] = dot(head_ref[...], f_ref[ri]).astype(BF)
    turns = [turn(idx_ref, chan) for chan in range(2)]
    for half, ref in enumerate((sig_ref, cot_ref)):
        x = ref[...]
        re = dot(x, t_ref[:, :HALF]).reshape(8, 2, ROWS, HALF)
        im = dot(x, t_ref[:, HALF:]).reshape(8, 2, ROWS, HALF)
        re, im = swap_first((re[:, 0], re[:, 1]), (im[:, 0], im[:, 1]))
        at = pl.ds(half * 128, 128)
        out_re = [re[c] * turns[c][0] - im[c] * turns[c][1] for c in range(2)]
        out_im = [re[c] * turns[c][1] + im[c] * turns[c][0] for c in range(2)]
        for y, v in ((yre, out_re), (yim, out_im)):
            v = jnp.stack(v, axis=1).reshape(128, HALF)
            for s in range(2):
                y[s, at, :] = v[:, s * 128 : (s + 1) * 128]
    for r in range(ROWS):
        rows = [y[s, pl.ds(r, 32, stride=ROWS), :] for y in (yre, yim) for s in range(2)]
        block = jnp.concatenate(rows, axis=0).T
        for p in range(2):
            z[p, pl.ds(r, 64, stride=ROWS), :] = block[p * 64 : (p + 1) * 64]
    for p in range(2):
        out_ref[:, p * 128 : (p + 1) * 128] = z[p].astype(BF)


def kernel_f(idx_ref, f_ref, tail_ref, head_ref, own_ref, mirror_ref, flip_ref, h_ref, rows):
    place = idx_ref[0]
    kind = jnp.where(place == 0, 0, jnp.where(place < 32, 1, 2))
    rows[:, :64, :] = f_ref[...]
    rows[:, 64:96, :] = tail_ref[...]
    rows[:, 96:, :] = jnp.zeros((2, 16, N), BF)
    rows[:, 96:104, :] = head_ref[...]
    lane = lax.broadcasted_iota(jnp.int32, (N, HALF), 1)
    shifted = ((lane & ~30) == 0) | ((lane & ~30) == 64)
    shifted = shifted & (place == 0)
    negative = ((lane >> 6) & 1) == ((lane >> 4) & 1)
    for ri in range(2):
        near = dot(rows[ri], own_ref[kind], ((0,), (0,)))
        far = dot(rows[ri], mirror_ref[kind], ((0,), (0,))).astype(BF)
        far = dot(flip_ref[...], far)
        far = jnp.where(shifted, pltpu.roll(far, 1, 0), far)
        if ri == 0:
            h_ref[:, :HALF] = near + far
        else:
            value = near - far
            h_ref[:, HALF:] = jnp.where(negative, -value, value)


def kernel_b(idx_ref, r_ref, wc_ref, ws_ref, h_ref, gather_ref, v_ref, g_ref, prod):
    first = jnp.where(idx_ref[0] == 0, 1, 0)
    sign = jnp.where(lax.broadcasted_iota(jnp.int32, (128, 128), 1) < 64, -1.0, 1.0)
    for k in range(4):
        at = pl.ds(k * 128, 128)
        p1 = dot(wc_ref[at, :], r_ref[...])
        p2 = dot(ws_ref[at, :], r_ref[...])
        pairs = []
        for p in range(2):
            cols = slice(p * 128, (p + 1) * 128)
            x = p1[:, cols] + sign * pltpu.roll(p2[:, cols], 64, 1)
            swapped = pltpu.roll(x, 64, 1)
            h1 = h_ref[at, p * 128 : (p + 1) * 128]
            h2 = h_ref[at, HALF + p * 128 : HALF + (p + 1) * 128]
            prod[at, cols] = (h1 * x + h2 * swapped).astype(BF)
            pairs.append((pltpu.roll(x, 112, 1) * x, pltpu.roll(x, 48, 1) * x))
        for ri in range(2):
            terms = jnp.concatenate([pairs[0][ri], pairs[1][ri]], axis=1)
            g_ref[ri, :, at] = dot(
                gather_ref[first, ri], terms, ((1,), (1,)), lax.Precision.HIGHEST
            ).astype(BF)
    for k in range(4):
        at = pl.ds(k * 128, 128)
        q1 = dot(wc_ref[at, :], prod[...])
        q2 = dot(ws_ref[at, :], prod[...])
        for p in range(2):
            cols = slice(p * 128, (p + 1) * 128)
            v_ref[at, cols] = (q1[:, cols] - sign * pltpu.roll(q2[:, cols], 64, 1)).astype(BF)


def kernel_c(idx_ref, v_ref, t_ref, out_ref, grad_ref, z, yre, yim):
    for p in range(2):
        z[p] = v_ref[:, p * 128 : (p + 1) * 128].astype(F32)
    for r in range(ROWS):
        rows = [z[p, pl.ds(r, 64, stride=ROWS), :] for p in range(2)]
        block = jnp.concatenate(rows, axis=0).T
        for ri, y in enumerate((yre, yim)):
            for s in range(2):
                at = ri * 64 + s * 32
                y[s, pl.ds(r, 32, stride=ROWS), :] = block[at : at + 32]
    double = jnp.where(lax.broadcasted_iota(jnp.int32, (ROWS, HALF), 1) == 0, 1.0, 2.0)
    turns = [[t * double for t in turn(idx_ref, chan)] for chan in range(2)]
    for half, ref in enumerate((out_ref, grad_ref)):
        at = pl.ds(half * 128, 128)
        re, im = (
            jnp.concatenate([y[s, at, :] for s in range(2)], axis=1).reshape(8, 2, ROWS, HALF)
            for y in (yre, yim)
        )
        mid_re = [re[:, c] * turns[c][0] + im[:, c] * turns[c][1] for c in range(2)]
        mid_im = [im[:, c] * turns[c][0] - re[:, c] * turns[c][1] for c in range(2)]
        mid_re, mid_im = (
            jnp.stack(v, axis=1).reshape(128, HALF).astype(BF) for v in swap_first(mid_re, mid_im)
        )
        total = dot(mid_re, t_ref[:, :HALF], ((1,), (1,)))
        total = total + dot(mid_im, t_ref[:, HALF:], ((1,), (1,)))
        ref[...] = total.astype(BF)


def kernel_g(idx_ref, g_ref, far_ref, head_ref, own_ref, mirror_ref, flip_ref, out_ref, rows):
    place = idx_ref[0]
    kind = jnp.where(
        place == 0, 0, jnp.where(place == 32, 3, jnp.where(place < 32, 1, 2))
    )
    rows[:, :48, :] = g_ref[...]
    rows[:, 48:80, :] = far_ref[...]
    rows[:, 80:96, :] = jnp.zeros((2, 16, N), BF)
    rows[:, 96:, :] = jnp.zeros((2, 16, N), BF)
    rows[:, 96:104, :] = head_ref[...]
    row = lax.broadcasted_iota(jnp.int32, (64, N), 0)
    shifted = ((row & 7) == 0) & (place == 0)
    for ri in range(2):
        near = dot(own_ref[kind], rows[ri])
        far = dot(mirror_ref[kind], rows[ri]).astype(BF)
        far = dot(far, flip_ref[...])
        far = jnp.where(shifted, pltpu.roll(far, 1, 1), far)
        out_ref[ri] = (near + far if ri == 0 else near - far).astype(BF)


def body(signal, cotangent, filter_spec):
    shape = signal.shape
    place = lax.axis_index("seq").astype(jnp.int32).reshape(1)
    table = jnp.asarray(first_table())
    cos_t, sin_t = (jnp.asarray(t) for t in unit_tables())
    flip = jnp.asarray(np.eye(N, dtype=np.float32)[::-1].astype(BF))
    tail, head = (jnp.asarray(t) for t in payload_selectors())
    f_own, f_mirror = (jnp.asarray(t) for t in filter_selectors())
    g_own, g_mirror = (jnp.asarray(t) for t in grad_selectors())
    gather = jnp.asarray(gather_tables())
    opposite = [(d, SEQ - 1 - d) for d in range(SEQ)]
    heads_to = [(d, {0: 32, 32: 0}.get(d, SEQ - d)) for d in range(SEQ)]
    filt = filter_spec.reshape(2, 64, N)
    sent, tails, heads = pl.pallas_call(
        kernel_a,
        in_specs=[SMEM] + [VMEM] * 6,
        out_specs=[VMEM] * 3,
        out_shape=[
            jax.ShapeDtypeStruct((N, HALF), BF),
            jax.ShapeDtypeStruct((2, 32, N), BF),
            jax.ShapeDtypeStruct((2, 8, N), BF),
        ],
        scratch_shapes=[
            pltpu.VMEM((2, 256, 128), F32),
            pltpu.VMEM((2, 256, 128), F32),
            pltpu.VMEM((2, N, 128), F32),
        ],
    )(place, signal.reshape(128, N), cotangent.reshape(128, N), table, filt, tail, head)
    got = lax.all_to_all(sent.reshape(SEQ, ROWS, HALF), "seq", 0, 0, tiled=True)
    tails = lax.ppermute(tails, "seq", opposite)
    heads = lax.ppermute(heads, "seq", heads_to)
    spread = pl.pallas_call(
        kernel_f,
        in_specs=[SMEM] + [VMEM] * 6,
        out_specs=VMEM,
        out_shape=jax.ShapeDtypeStruct((N, N), F32),
        scratch_shapes=[pltpu.VMEM((2, 112, N), BF)],
        compiler_params=PARAMS,
        cost_estimate=pl.CostEstimate(flops=400000000, bytes_accessed=2000000, transcendentals=0),
    )(place, filt, tails, heads, f_own, f_mirror, flip)
    back, grad = pl.pallas_call(
        kernel_b,
        in_specs=[SMEM] + [VMEM] * 5,
        out_specs=[VMEM, VMEM],
        out_shape=[
            jax.ShapeDtypeStruct((N, HALF), BF),
            jax.ShapeDtypeStruct((2, 48, N), BF),
        ],
        scratch_shapes=[pltpu.VMEM((N, HALF), BF)],
        compiler_params=PARAMS,
    )(place, got.reshape(N, HALF), cos_t, sin_t, spread, gather)
    mid = lax.all_to_all(back.reshape(SEQ, ROWS, HALF), "seq", 0, 0, tiled=True)
    for bit in (1, 2, 4):
        other = lax.ppermute(grad, "dp", [(d, d ^ bit) for d in range(8)])
        grad = (grad.astype(F32) + other.astype(F32)).astype(BF)
    far = lax.ppermute(grad[:, :32], "seq", opposite)
    slot = jnp.where(place[0] == 0, grad[:, 32:40], grad[:, :8])
    slot = lax.ppermute(slot, "seq", heads_to)
    output, grad_signal = pl.pallas_call(
        kernel_c,
        in_specs=[SMEM, VMEM, VMEM],
        out_specs=[VMEM, VMEM],
        out_shape=[jax.ShapeDtypeStruct((128, N), BF)] * 2,
        scratch_shapes=[
            pltpu.VMEM((2, N, 128), F32),
            pltpu.VMEM((2, 256, 128), F32),
            pltpu.VMEM((2, 256, 128), F32),
        ],
        compiler_params=PARAMS,
        cost_estimate=pl.CostEstimate(flops=400000000, bytes_accessed=2000000, transcendentals=0),
    )(place, mid.reshape(N, HALF), table)
    grad_filter = pl.pallas_call(
        kernel_g,
        in_specs=[SMEM] + [VMEM] * 6,
        out_specs=VMEM,
        out_shape=jax.ShapeDtypeStruct((2, 64, N), BF),
        scratch_shapes=[pltpu.VMEM((2, 112, N), BF)],
        compiler_params=PARAMS,
        cost_estimate=pl.CostEstimate(flops=100000000, bytes_accessed=1000000, transcendentals=0),
    )(place, grad, far, slot, g_own, g_mirror, flip)
    return output.reshape(shape), grad_signal.reshape(shape), grad_filter.reshape(2, 8, 8, N)


def solution(mesh):
    placed = (P(None, "dp", "seq", None), P(None, "dp", "seq", None), P(None, None, "seq", None))
    return jax.shard_map(body, mesh=mesh, in_specs=placed, out_specs=placed, check_vma=False)
```

```python
import math

import jax
import jax.numpy as jnp
import numpy as np
from jax import lax
from jax.experimental import pallas as pl
from jax.experimental.pallas import tpu as pltpu
from jax.sharding import PartitionSpec as P

N = 512
SEQ = 64
ROWS = N // SEQ
HALF = N // 2
BF = jnp.bfloat16
F32 = jnp.float32
VMEM = pl.BlockSpec(memory_space=pltpu.VMEM)
SMEM = pl.BlockSpec(memory_space=pltpu.SMEM)
PARAMS = pltpu.CompilerParams(vmem_limit_bytes=20 * 2**20)


def unit_tables():
    steps = np.arange(N, dtype=np.int32)
    phases = (steps[:, None] * steps[None, :] % N).astype(np.float32) * np.float32(
        2.0 * math.pi / N
    )
    factor = np.float32(1.0 / math.sqrt(N))
    return (np.cos(phases) * factor).astype(BF), (-np.sin(phases) * factor).astype(BF)


def first_table():
    cos_t, sin_t = unit_tables()
    col = np.arange(HALF)
    place = col % 64
    row = 8 * place + 2 * (col // 128) + col // 64 % 2 + (place >= 32)
    re, im = cos_t[:, row], sin_t[:, row]
    im[:, 0] = cos_t[:, HALF]
    return np.concatenate([re, im], axis=1)


def lanes():
    lane = np.arange(HALF)
    slot = 2 * (lane // 32 % 2) + lane // 128
    return slot, lane // 64 % 2, lane // 16 % 2, lane // 2 % 8, lane % 2


def filter_selectors():
    slot, _, _, filt, chan = lanes()
    own = np.zeros((3, 112, HALF), np.float32)
    mirror = np.zeros((3, 112, HALF), np.float32)
    for lane in range(HALF):
        k, f = slot[lane], filt[lane]
        for kind in (0, 1):
            own[kind, f * 8 + k, lane] = 0.5
            mirror[kind, 96 + f if k == 0 else 64 + f * 4 + 4 - k, lane] = 0.5
        own[2, f * 8 + k + 1, lane] = 0.5
        mirror[2, 64 + f * 4 + 3 - k, lane] = 0.5
        if k == 0:
            own[0, :, lane] = 0
            mirror[0, :, lane] = 0
            source = 96 + f if chan[lane] else f * 8
            own[0, source, lane] = 0.5
            mirror[0, source, lane] = 0.5
    return own.astype(BF), mirror.astype(BF)


def gather_tables():
    slot, part, kind, filt, chan = lanes()
    out = np.zeros((2, 2, 48, HALF), np.float32)
    for lane in range(HALF):
        if kind[lane]:
            continue
        for first in range(2):
            for ri in range(2):
                sign = -1.0 if ri and part[lane] else 1.0
                extra = slot[lane] == 0 and chan[lane] == 1
                if not (first and extra):
                    out[first, ri, slot[lane] * 8 + filt[lane], lane] = sign
                if extra:
                    out[first, ri, 32 + filt[lane], lane] = sign
    return out.astype(BF)


def grad_selectors():
    own = np.zeros((4, 64, 112), np.float32)
    mirror = np.zeros((4, 64, 112), np.float32)
    for f in range(8):
        for row in range(8):
            at = f * 8 + row
            for kind in (0, 1):
                if row < 4:
                    own[kind, at, row * 8 + f] = 1
                else:
                    mirror[kind, at, 48 + (7 - row) * 8 + f] = 1
            for kind in (2, 3):
                if row == 0:
                    mirror[kind, at, 96 + f] = 1
                elif row < 5:
                    own[kind, at, (row - 1) * 8 + f] = 1
                else:
                    mirror[kind, at, 48 + (8 - row) * 8 + f] = 1
        own[0, f * 8, f] = 0.5
        mirror[0, f * 8, f] = 0.5
        own[3, f * 8, 96 + f] = 0.5
        mirror[3, f * 8, 96 + f] = 0.5
    return own.astype(BF), mirror.astype(BF)


def payload_selectors():
    tail = np.zeros((32, 64), np.float32)
    head = np.zeros((8, 64), np.float32)
    for f in range(8):
        head[f, f * 8] = 1
        for row in range(4):
            tail[f * 4 + row, f * 8 + 4 + row] = 1
    return tail.astype(BF), head.astype(BF)


def dot(a, b, dims=((1,), (0,)), precision=None):
    return lax.dot_general(a, b, (dims, ((), ())), precision=precision, preferred_element_type=F32)


def turn(idx_ref, chan):
    shape = (ROWS, HALF)
    lane = lax.broadcasted_iota(jnp.int32, shape, 1)
    row = idx_ref[0] * ROWS + lax.broadcasted_iota(jnp.int32, shape, 0)
    place = lane & 63
    col = 8 * place + 2 * (lane >> 7) + ((lane >> 6) & 1) + (place >> 5)
    if chan:
        col = jnp.where(lane == 0, HALF, col)
    phases = (row * col).astype(F32) * (-2.0 * math.pi / (N * N))
    return jnp.cos(phases), jnp.sin(phases)


def swap_first(re, im):
    first = lax.broadcasted_iota(jnp.int32, re[0].shape, 2) == 0
    return (re[0], jnp.where(first, im[0], re[1])), (jnp.where(first, re[1], im[0]), im[1])


def kernel_a(idx_ref, sig_ref, cot_ref, t_ref, f_ref, tail_ref, head_ref, out_ref, tails_ref,
             heads_ref, yre, yim, z):
    for ri in range(2):
        tails_ref[ri] = dot(tail_ref[...], f_ref[ri]).astype(BF)
        heads_ref[ri] = dot(head_ref[...], f_ref[ri]).astype(BF)
    turns = [turn(idx_ref, chan) for chan in range(2)]
    for half, ref in enumerate((sig_ref, cot_ref)):
        x = ref[...]
        re = dot(x, t_ref[:, :HALF]).reshape(8, 2, ROWS, HALF)
        im = dot(x, t_ref[:, HALF:]).reshape(8, 2, ROWS, HALF)
        re, im = swap_first((re[:, 0], re[:, 1]), (im[:, 0], im[:, 1]))
        at = pl.ds(half * 128, 128)
        out_re = [re[c] * turns[c][0] - im[c] * turns[c][1] for c in range(2)]
        out_im = [re[c] * turns[c][1] + im[c] * turns[c][0] for c in range(2)]
        for y, v in ((yre, out_re), (yim, out_im)):
            v = jnp.stack(v, axis=1).reshape(128, HALF)
            for s in range(2):
                y[s, at, :] = v[:, s * 128 : (s + 1) * 128]
    for r in range(ROWS):
        rows = [y[s, pl.ds(r, 32, stride=ROWS), :] for y in (yre, yim) for s in range(2)]
        block = jnp.concatenate(rows, axis=0).T
        for p in range(2):
            z[p, pl.ds(r, 64, stride=ROWS), :] = block[p * 64 : (p + 1) * 64]
    for p in range(2):
        out_ref[:, p * 128 : (p + 1) * 128] = z[p].astype(BF)


def kernel_f(idx_ref, f_ref, tail_ref, head_ref, own_ref, mirror_ref, flip_ref, h_ref, rows):
    place = idx_ref[0]
    kind = jnp.where(place == 0, 0, jnp.where(place < 32, 1, 2))
    rows[:, :64, :] = f_ref[...]
    rows[:, 64:96, :] = tail_ref[...]
    rows[:, 96:, :] = jnp.zeros((2, 16, N), BF)
    rows[:, 96:104, :] = head_ref[...]
    lane = lax.broadcasted_iota(jnp.int32, (N, HALF), 1)
    shifted = ((lane & ~30) == 0) | ((lane & ~30) == 64)
    shifted = shifted & (place == 0)
    negative = ((lane >> 6) & 1) == ((lane >> 4) & 1)
    for ri in range(2):
        near = dot(rows[ri], own_ref[kind], ((0,), (0,)))
        far = dot(rows[ri], mirror_ref[kind], ((0,), (0,))).astype(BF)
        far = dot(flip_ref[...], far)
        far = jnp.where(shifted, pltpu.roll(far, 1, 0), far)
        if ri == 0:
            h_ref[:, :HALF] = near + far
        else:
            value = near - far
            h_ref[:, HALF:] = jnp.where(negative, -value, value)


def kernel_b(idx_ref, r_ref, wc_ref, ws_ref, h_ref, gather_ref, v_ref, g_ref, prod):
    first = jnp.where(idx_ref[0] == 0, 1, 0)
    sign = jnp.where(lax.broadcasted_iota(jnp.int32, (128, 128), 1) < 64, -1.0, 1.0)
    for k in range(4):
        at = pl.ds(k * 128, 128)
        p1 = dot(wc_ref[at, :], r_ref[...])
        p2 = dot(ws_ref[at, :], r_ref[...])
        pairs = []
        for p in range(2):
            cols = slice(p * 128, (p + 1) * 128)
            x = p1[:, cols] + sign * pltpu.roll(p2[:, cols], 64, 1)
            swapped = pltpu.roll(x, 64, 1)
            h1 = h_ref[at, p * 128 : (p + 1) * 128]
            h2 = h_ref[at, HALF + p * 128 : HALF + (p + 1) * 128]
            prod[at, cols] = (h1 * x + h2 * swapped).astype(BF)
            pairs.append((pltpu.roll(x, 112, 1) * x, pltpu.roll(x, 48, 1) * x))
        for ri in range(2):
            terms = jnp.concatenate([pairs[0][ri], pairs[1][ri]], axis=1)
            high = terms.astype(BF)
            low = (terms - high.astype(F32)).astype(BF)
            take = gather_ref[first, ri]
            total = dot(take, high, ((1,), (1,))) + dot(take, low, ((1,), (1,)))
            g_ref[ri, :, at] = total.astype(BF)
    for k in range(4):
        at = pl.ds(k * 128, 128)
        q1 = dot(wc_ref[at, :], prod[...])
        q2 = dot(ws_ref[at, :], prod[...])
        for p in range(2):
            cols = slice(p * 128, (p + 1) * 128)
            v_ref[at, cols] = (q1[:, cols] - sign * pltpu.roll(q2[:, cols], 64, 1)).astype(BF)


def kernel_c(idx_ref, v_ref, t_ref, out_ref, grad_ref, z, yre, yim):
    for p in range(2):
        z[p] = v_ref[:, p * 128 : (p + 1) * 128].astype(F32)
    for r in range(ROWS):
        rows = [z[p, pl.ds(r, 64, stride=ROWS), :] for p in range(2)]
        block = jnp.concatenate(rows, axis=0).T
        for ri, y in enumerate((yre, yim)):
            for s in range(2):
                at = ri * 64 + s * 32
                y[s, pl.ds(r, 32, stride=ROWS), :] = block[at : at + 32]
    double = jnp.where(lax.broadcasted_iota(jnp.int32, (ROWS, HALF), 1) == 0, 1.0, 2.0)
    turns = [[t * double for t in turn(idx_ref, chan)] for chan in range(2)]
    for half, ref in enumerate((out_ref, grad_ref)):
        at = pl.ds(half * 128, 128)
        re, im = (
            jnp.concatenate([y[s, at, :] for s in range(2)], axis=1).reshape(8, 2, ROWS, HALF)
            for y in (yre, yim)
        )
        mid_re = [re[:, c] * turns[c][0] + im[:, c] * turns[c][1] for c in range(2)]
        mid_im = [im[:, c] * turns[c][0] - re[:, c] * turns[c][1] for c in range(2)]
        mid_re, mid_im = (
            jnp.stack(v, axis=1).reshape(128, HALF).astype(BF) for v in swap_first(mid_re, mid_im)
        )
        total = dot(mid_re, t_ref[:, :HALF], ((1,), (1,)))
        total = total + dot(mid_im, t_ref[:, HALF:], ((1,), (1,)))
        ref[...] = total.astype(BF)


def kernel_g(idx_ref, g_ref, far_ref, head_ref, own_ref, mirror_ref, flip_ref, out_ref, rows):
    place = idx_ref[0]
    kind = jnp.where(
        place == 0, 0, jnp.where(place == 32, 3, jnp.where(place < 32, 1, 2))
    )
    rows[:, :48, :] = g_ref[...]
    rows[:, 48:80, :] = far_ref[...]
    rows[:, 80:96, :] = jnp.zeros((2, 16, N), BF)
    rows[:, 96:, :] = jnp.zeros((2, 16, N), BF)
    rows[:, 96:104, :] = head_ref[...]
    row = lax.broadcasted_iota(jnp.int32, (64, N), 0)
    shifted = ((row & 7) == 0) & (place == 0)
    for ri in range(2):
        near = dot(own_ref[kind], rows[ri])
        far = dot(mirror_ref[kind], rows[ri]).astype(BF)
        far = dot(far, flip_ref[...])
        far = jnp.where(shifted, pltpu.roll(far, 1, 1), far)
        out_ref[ri] = (near + far if ri == 0 else near - far).astype(BF)


def body(signal, cotangent, filter_spec):
    shape = signal.shape
    place = lax.axis_index("seq").astype(jnp.int32).reshape(1)
    table = jnp.asarray(first_table())
    cos_t, sin_t = (jnp.asarray(t) for t in unit_tables())
    flip = jnp.asarray(np.eye(N, dtype=np.float32)[::-1].astype(BF))
    tail, head = (jnp.asarray(t) for t in payload_selectors())
    f_own, f_mirror = (jnp.asarray(t) for t in filter_selectors())
    g_own, g_mirror = (jnp.asarray(t) for t in grad_selectors())
    gather = jnp.asarray(gather_tables())
    opposite = [(d, SEQ - 1 - d) for d in range(SEQ)]
    heads_to = [(d, {0: 32, 32: 0}.get(d, SEQ - d)) for d in range(SEQ)]
    filt = filter_spec.reshape(2, 64, N)
    sent, tails, heads = pl.pallas_call(
        kernel_a,
        in_specs=[SMEM] + [VMEM] * 6,
        out_specs=[VMEM] * 3,
        out_shape=[
            jax.ShapeDtypeStruct((N, HALF), BF),
            jax.ShapeDtypeStruct((2, 32, N), BF),
            jax.ShapeDtypeStruct((2, 8, N), BF),
        ],
        scratch_shapes=[
            pltpu.VMEM((2, 256, 128), F32),
            pltpu.VMEM((2, 256, 128), F32),
            pltpu.VMEM((2, N, 128), F32),
        ],
    )(place, signal.reshape(128, N), cotangent.reshape(128, N), table, filt, tail, head)
    got = lax.all_to_all(sent.reshape(SEQ, ROWS, HALF), "seq", 0, 0, tiled=True)
    tails = lax.ppermute(tails, "seq", opposite)
    heads = lax.ppermute(heads, "seq", heads_to)
    spread = pl.pallas_call(
        kernel_f,
        in_specs=[SMEM] + [VMEM] * 6,
        out_specs=VMEM,
        out_shape=jax.ShapeDtypeStruct((N, N), F32),
        scratch_shapes=[pltpu.VMEM((2, 112, N), BF)],
        compiler_params=PARAMS,
        cost_estimate=pl.CostEstimate(flops=400000000, bytes_accessed=2000000, transcendentals=0),
    )(place, filt, tails, heads, f_own, f_mirror, flip)
    back, grad = pl.pallas_call(
        kernel_b,
        in_specs=[SMEM] + [VMEM] * 5,
        out_specs=[VMEM, VMEM],
        out_shape=[
            jax.ShapeDtypeStruct((N, HALF), BF),
            jax.ShapeDtypeStruct((2, 48, N), BF),
        ],
        scratch_shapes=[pltpu.VMEM((N, HALF), BF)],
        compiler_params=PARAMS,
    )(place, got.reshape(N, HALF), cos_t, sin_t, spread, gather)
    far = lax.ppermute(grad[:, :32], "seq", opposite)
    slot = jnp.where(place[0] == 0, grad[:, 32:40], grad[:, :8])
    slot = lax.ppermute(slot, "seq", heads_to)
    mid = lax.all_to_all(back.reshape(SEQ, ROWS, HALF), "seq", 0, 0, tiled=True)
    grad = pl.pallas_call(
        kernel_g,
        in_specs=[SMEM] + [VMEM] * 6,
        out_specs=VMEM,
        out_shape=jax.ShapeDtypeStruct((2, 64, N), BF),
        scratch_shapes=[pltpu.VMEM((2, 112, N), BF)],
        compiler_params=PARAMS,
        cost_estimate=pl.CostEstimate(flops=100000000, bytes_accessed=1000000, transcendentals=0),
    )(place, grad, far, slot, g_own, g_mirror, flip)
    for bit in (2, 4, 1):
        other = lax.ppermute(grad, "dp", [(d, d ^ bit) for d in range(8)])
        grad = (grad.astype(F32) + other.astype(F32)).astype(BF)
    output, grad_signal = pl.pallas_call(
        kernel_c,
        in_specs=[SMEM, VMEM, VMEM],
        out_specs=[VMEM, VMEM],
        out_shape=[jax.ShapeDtypeStruct((128, N), BF)] * 2,
        scratch_shapes=[
            pltpu.VMEM((2, N, 128), F32),
            pltpu.VMEM((2, 256, 128), F32),
            pltpu.VMEM((2, 256, 128), F32),
        ],
        compiler_params=PARAMS,
        cost_estimate=pl.CostEstimate(flops=400000000, bytes_accessed=2000000, transcendentals=0),
    )(place, mid.reshape(N, HALF), table)
    return output.reshape(shape), grad_signal.reshape(shape), grad.reshape(2, 8, 8, N)


def solution(mesh):
    placed = (P(None, "dp", "seq", None), P(None, "dp", "seq", None), P(None, None, "seq", None))
    return jax.shard_map(body, mesh=mesh, in_specs=placed, out_specs=placed, check_vma=False)
```

```python
import math

import jax
import jax.numpy as jnp
import numpy as np
from jax import lax
from jax.experimental import pallas as pl
from jax.experimental.pallas import tpu as pltpu
from jax.sharding import PartitionSpec as P

N = 512
SEQ = 64
ROWS = N // SEQ
HALF = N // 2
BF = jnp.bfloat16
F32 = jnp.float32
VMEM = pl.BlockSpec(memory_space=pltpu.VMEM)
SMEM = pl.BlockSpec(memory_space=pltpu.SMEM)
PARAMS = pltpu.CompilerParams(vmem_limit_bytes=20 * 2**20)


def unit_tables():
    steps = np.arange(N, dtype=np.int32)
    phases = (steps[:, None] * steps[None, :] % N).astype(np.float32) * np.float32(
        2.0 * math.pi / N
    )
    factor = np.float32(1.0 / math.sqrt(N))
    return (np.cos(phases) * factor).astype(BF), (-np.sin(phases) * factor).astype(BF)


def first_table():
    cos_t, sin_t = unit_tables()
    col = np.arange(HALF)
    place = col % 64
    row = 8 * place + 2 * (col // 128) + col // 64 % 2 + (place >= 32)
    re, im = cos_t[:, row], sin_t[:, row]
    im[:, 0] = cos_t[:, HALF]
    return np.concatenate([re, im], axis=1)


def lanes():
    lane = np.arange(HALF)
    slot = 2 * (lane // 32 % 2) + lane // 128
    return slot, lane // 64 % 2, lane // 16 % 2, lane // 2 % 8, lane % 2


def tail_row(f, row):
    return 64 + 16 * (f // 2) + 4 * (f % 2) + row - 4


def head_row(f):
    return 72 + 16 * (f // 2) + f % 2


def filter_selectors():
    slot, _, _, filt, chan = lanes()
    own = np.zeros((3, 128, HALF), np.float32)
    mirror = np.zeros((3, 128, HALF), np.float32)
    for lane in range(HALF):
        k, f = slot[lane], filt[lane]
        for kind in (0, 1):
            own[kind, f * 8 + k, lane] = 0.5
            mirror[kind, head_row(f) if k == 0 else tail_row(f, 8 - k), lane] = 0.5
        own[2, f * 8 + k + 1, lane] = 0.5
        mirror[2, tail_row(f, 7 - k), lane] = 0.5
        if k == 0:
            own[0, :, lane] = 0
            mirror[0, :, lane] = 0
            source = head_row(f) if chan[lane] else f * 8
            own[0, source, lane] = 0.5
            mirror[0, source, lane] = 0.5
    return own.astype(BF), mirror.astype(BF)


def gather_tables():
    slot, part, kind, filt, chan = lanes()
    out = np.zeros((2, 2, 48, HALF), np.float32)
    for lane in range(HALF):
        if kind[lane]:
            continue
        for first in range(2):
            for ri in range(2):
                sign = -1.0 if ri and part[lane] else 1.0
                extra = slot[lane] == 0 and chan[lane] == 1
                if not (first and extra):
                    out[first, ri, slot[lane] * 8 + filt[lane], lane] = sign
                if extra:
                    out[first, ri, 32 + filt[lane], lane] = sign
    return out.astype(BF)


def grad_selectors():
    own = np.zeros((4, 64, 112), np.float32)
    mirror = np.zeros((4, 64, 112), np.float32)
    for f in range(8):
        for row in range(8):
            at = f * 8 + row
            for kind in (0, 1):
                if row < 4:
                    own[kind, at, row * 8 + f] = 1
                else:
                    mirror[kind, at, 48 + (7 - row) * 8 + f] = 1
            for kind in (2, 3):
                if row == 0:
                    mirror[kind, at, 96 + f] = 1
                elif row < 5:
                    own[kind, at, (row - 1) * 8 + f] = 1
                else:
                    mirror[kind, at, 48 + (8 - row) * 8 + f] = 1
        own[0, f * 8, f] = 0.5
        mirror[0, f * 8, f] = 0.5
        own[3, f * 8, 96 + f] = 0.5
        mirror[3, f * 8, 96 + f] = 0.5
    return own.astype(BF), mirror.astype(BF)


def payload_selectors():
    out = np.zeros((2, 4, 8, 64), np.float32)
    for f in range(8):
        out[1, f // 2, f % 2, f * 8] = 1
        for row in range(4):
            out[0, f // 2, 4 * (f % 2) + row, f * 8 + 4 + row] = 1
    return out.astype(BF)


def dot(a, b, dims=((1,), (0,)), precision=None):
    return lax.dot_general(a, b, (dims, ((), ())), precision=precision, preferred_element_type=F32)


def turn(idx_ref, chan):
    shape = (ROWS, HALF)
    lane = lax.broadcasted_iota(jnp.int32, shape, 1)
    row = idx_ref[0] * ROWS + lax.broadcasted_iota(jnp.int32, shape, 0)
    place = lane & 63
    col = 8 * place + 2 * (lane >> 7) + ((lane >> 6) & 1) + (place >> 5)
    if chan:
        col = jnp.where(lane == 0, HALF, col)
    phases = (row * col).astype(F32) * (-2.0 * math.pi / (N * N))
    return jnp.cos(phases), jnp.sin(phases)


def swap_first(re, im):
    first = lax.broadcasted_iota(jnp.int32, re[0].shape, 2) == 0
    return (re[0], jnp.where(first, im[0], re[1])), (jnp.where(first, re[1], im[0]), im[1])


def kernel_a(idx_ref, rank_ref, sig_ref, cot_ref, t_ref, f_ref, pick_ref, out_ref, tails_ref, heads_ref,
             yre, yim, z):
    pair = rank_ref[0] >> 1
    for ri in range(2):
        tails_ref[ri] = dot(pick_ref[0, pair], f_ref[ri]).astype(BF)
        heads_ref[ri] = dot(pick_ref[1, pair], f_ref[ri]).astype(BF)
    turns = [turn(idx_ref, chan) for chan in range(2)]
    for half, ref in enumerate((sig_ref, cot_ref)):
        x = ref[...]
        re = dot(x, t_ref[:, :HALF]).reshape(8, 2, ROWS, HALF)
        im = dot(x, t_ref[:, HALF:]).reshape(8, 2, ROWS, HALF)
        re, im = swap_first((re[:, 0], re[:, 1]), (im[:, 0], im[:, 1]))
        at = pl.ds(half * 128, 128)
        out_re = [re[c] * turns[c][0] - im[c] * turns[c][1] for c in range(2)]
        out_im = [re[c] * turns[c][1] + im[c] * turns[c][0] for c in range(2)]
        for y, v in ((yre, out_re), (yim, out_im)):
            v = jnp.stack(v, axis=1).reshape(128, HALF)
            for s in range(2):
                y[s, at, :] = v[:, s * 128 : (s + 1) * 128]
    for r in range(ROWS):
        rows = [y[s, pl.ds(r, 32, stride=ROWS), :] for y in (yre, yim) for s in range(2)]
        block = jnp.concatenate(rows, axis=0).T
        for p in range(2):
            z[p, pl.ds(r, 64, stride=ROWS), :] = block[p * 64 : (p + 1) * 64]
    for p in range(2):
        out_ref[:, p * 128 : (p + 1) * 128] = z[p].astype(BF)


def kernel_f(idx_ref, rank_ref, f_ref, s0_ref, s1_ref, s2_ref, s3_ref, own_ref, mirror_ref, flip_ref, h_ref, rows):
    place = idx_ref[0]
    kind = jnp.where(place == 0, 0, jnp.where(place < 32, 1, 2))
    rows[:, :64, :] = f_ref[...]
    for k, share_ref in enumerate((s0_ref, s1_ref, s2_ref, s3_ref)):
        at = pl.multiple_of(64 + 16 * ((rank_ref[0] >> 1) ^ k), 16)
        rows[:, pl.ds(at, 16), :] = share_ref[...]
    lane = lax.broadcasted_iota(jnp.int32, (N, HALF), 1)
    shifted = ((lane & ~30) == 0) | ((lane & ~30) == 64)
    shifted = shifted & (place == 0)
    negative = ((lane >> 6) & 1) == ((lane >> 4) & 1)
    for ri in range(2):
        near = dot(rows[ri], own_ref[kind], ((0,), (0,)))
        far = dot(rows[ri], mirror_ref[kind], ((0,), (0,))).astype(BF)
        far = dot(flip_ref[...], far)
        far = jnp.where(shifted, pltpu.roll(far, 1, 0), far)
        if ri == 0:
            h_ref[:, :HALF] = near + far
        else:
            value = near - far
            h_ref[:, HALF:] = jnp.where(negative, -value, value)


def signs():
    return jnp.where(lax.broadcasted_iota(jnp.int32, (128, 128), 1) < 64, -1.0, 1.0)


def kernel_b(idx_ref, r_ref, wc_ref, ws_ref, gather_ref, x_ref, g_ref):
    first = jnp.where(idx_ref[0] == 0, 1, 0)
    sign = signs()
    for k in range(4):
        at = pl.ds(k * 128, 128)
        p1 = dot(wc_ref[at, :], r_ref[...])
        p2 = dot(ws_ref[at, :], r_ref[...])
        pairs = []
        for p in range(2):
            cols = slice(p * 128, (p + 1) * 128)
            x = p1[:, cols] + sign * pltpu.roll(p2[:, cols], 64, 1)
            x_ref[at, cols] = x
            pairs.append((pltpu.roll(x, 112, 1) * x, pltpu.roll(x, 48, 1) * x))
        for ri in range(2):
            terms = jnp.concatenate([pairs[0][ri], pairs[1][ri]], axis=1)
            high = terms.astype(BF)
            low = (terms - high.astype(F32)).astype(BF)
            take = gather_ref[first, ri]
            total = dot(take, high, ((1,), (1,))) + dot(take, low, ((1,), (1,)))
            g_ref[ri, :, at] = total.astype(BF)


def kernel_d(x_ref, wc_ref, ws_ref, h_ref, v_ref, prod):
    sign = signs()
    for k in range(4):
        at = pl.ds(k * 128, 128)
        for p in range(2):
            cols = slice(p * 128, (p + 1) * 128)
            x = x_ref[at, cols]
            h1 = h_ref[at, cols]
            h2 = h_ref[at, HALF + p * 128 : HALF + (p + 1) * 128]
            prod[at, cols] = (h1 * x + h2 * pltpu.roll(x, 64, 1)).astype(BF)
    for k in range(4):
        at = pl.ds(k * 128, 128)
        q1 = dot(wc_ref[at, :], prod[...])
        q2 = dot(ws_ref[at, :], prod[...])
        for p in range(2):
            cols = slice(p * 128, (p + 1) * 128)
            v_ref[at, cols] = (q1[:, cols] - sign * pltpu.roll(q2[:, cols], 64, 1)).astype(BF)


def kernel_c(idx_ref, v_ref, t_ref, out_ref, grad_ref, z, yre, yim):
    for p in range(2):
        z[p] = v_ref[:, p * 128 : (p + 1) * 128].astype(F32)
    for r in range(ROWS):
        rows = [z[p, pl.ds(r, 64, stride=ROWS), :] for p in range(2)]
        block = jnp.concatenate(rows, axis=0).T
        for ri, y in enumerate((yre, yim)):
            for s in range(2):
                at = ri * 64 + s * 32
                y[s, pl.ds(r, 32, stride=ROWS), :] = block[at : at + 32]
    double = jnp.where(lax.broadcasted_iota(jnp.int32, (ROWS, HALF), 1) == 0, 1.0, 2.0)
    turns = [[t * double for t in turn(idx_ref, chan)] for chan in range(2)]
    for half, ref in enumerate((out_ref, grad_ref)):
        at = pl.ds(half * 128, 128)
        re, im = (
            jnp.concatenate([y[s, at, :] for s in range(2)], axis=1).reshape(8, 2, ROWS, HALF)
            for y in (yre, yim)
        )
        mid_re = [re[:, c] * turns[c][0] + im[:, c] * turns[c][1] for c in range(2)]
        mid_im = [im[:, c] * turns[c][0] - re[:, c] * turns[c][1] for c in range(2)]
        mid_re, mid_im = (
            jnp.stack(v, axis=1).reshape(128, HALF).astype(BF) for v in swap_first(mid_re, mid_im)
        )
        total = dot(mid_re, t_ref[:, :HALF], ((1,), (1,)))
        total = total + dot(mid_im, t_ref[:, HALF:], ((1,), (1,)))
        ref[...] = total.astype(BF)


def kernel_g(idx_ref, g_ref, far_ref, head_ref, own_ref, mirror_ref, flip_ref, out_ref, rows):
    place = idx_ref[0]
    kind = jnp.where(
        place == 0, 0, jnp.where(place == 32, 3, jnp.where(place < 32, 1, 2))
    )
    rows[:, :48, :] = g_ref[...]
    rows[:, 48:80, :] = far_ref[...]
    rows[:, 80:96, :] = jnp.zeros((2, 16, N), BF)
    rows[:, 96:, :] = jnp.zeros((2, 16, N), BF)
    rows[:, 96:104, :] = head_ref[...]
    row = lax.broadcasted_iota(jnp.int32, (64, N), 0)
    shifted = ((row & 7) == 0) & (place == 0)
    for ri in range(2):
        near = dot(own_ref[kind], rows[ri])
        far = dot(mirror_ref[kind], rows[ri]).astype(BF)
        far = dot(far, flip_ref[...])
        far = jnp.where(shifted, pltpu.roll(far, 1, 1), far)
        out_ref[ri] = (near + far if ri == 0 else near - far).astype(BF)


def body(signal, cotangent, filter_spec):
    shape = signal.shape
    place = lax.axis_index("seq").astype(jnp.int32).reshape(1)
    rank = lax.axis_index("dp").astype(jnp.int32).reshape(1)
    table = jnp.asarray(first_table())
    cos_t, sin_t = (jnp.asarray(t) for t in unit_tables())
    flip = jnp.asarray(np.eye(N, dtype=np.float32)[::-1].astype(BF))
    pick = jnp.asarray(payload_selectors())
    f_own, f_mirror = (jnp.asarray(t) for t in filter_selectors())
    g_own, g_mirror = (jnp.asarray(t) for t in grad_selectors())
    gather = jnp.asarray(gather_tables())
    opposite = [(d, SEQ - 1 - d) for d in range(SEQ)]
    heads_to = [(d, {0: 32, 32: 0}.get(d, SEQ - d)) for d in range(SEQ)]
    filt = filter_spec.reshape(2, 64, N)
    sent, tails, heads = pl.pallas_call(
        kernel_a,
        in_specs=[SMEM] * 2 + [VMEM] * 5,
        out_specs=[VMEM] * 3,
        out_shape=[
            jax.ShapeDtypeStruct((N, HALF), BF),
            jax.ShapeDtypeStruct((2, 8, N), BF),
            jax.ShapeDtypeStruct((2, 8, N), BF),
        ],
        scratch_shapes=[
            pltpu.VMEM((2, 256, 128), F32),
            pltpu.VMEM((2, 256, 128), F32),
            pltpu.VMEM((2, N, 128), F32),
        ],
    )(place, rank, signal.reshape(128, N), cotangent.reshape(128, N), table, filt, pick)
    got = lax.all_to_all(sent.reshape(SEQ, ROWS, HALF), "seq", 0, 0, tiled=True)
    tails = lax.ppermute(tails, "seq", opposite)
    heads = lax.ppermute(heads, "seq", heads_to)
    share = jnp.concatenate([tails, heads], axis=1)
    shares = [share] + [
        lax.ppermute(share, "dp", [(d, d ^ bit) for d in range(8)]) for bit in (2, 4, 6)
    ]
    spec, grad = pl.pallas_call(
        kernel_b,
        in_specs=[SMEM] + [VMEM] * 4,
        out_specs=[VMEM, VMEM],
        out_shape=[
            jax.ShapeDtypeStruct((N, HALF), F32),
            jax.ShapeDtypeStruct((2, 48, N), BF),
        ],
        compiler_params=PARAMS,
    )(place, got.reshape(N, HALF), cos_t, sin_t, gather)
    spread = pl.pallas_call(
        kernel_f,
        in_specs=[SMEM] * 2 + [VMEM] * 8,
        out_specs=VMEM,
        out_shape=jax.ShapeDtypeStruct((N, N), F32),
        scratch_shapes=[pltpu.VMEM((2, 128, N), BF)],
        compiler_params=PARAMS,
        cost_estimate=pl.CostEstimate(flops=400000000, bytes_accessed=2000000, transcendentals=0),
    )(place, rank, filt, *shares, f_own, f_mirror, flip)
    back = pl.pallas_call(
        kernel_d,
        in_specs=[VMEM] * 4,
        out_specs=VMEM,
        out_shape=jax.ShapeDtypeStruct((N, HALF), BF),
        scratch_shapes=[pltpu.VMEM((N, HALF), BF)],
        compiler_params=PARAMS,
    )(spec, cos_t, sin_t, spread)
    far = lax.ppermute(grad[:, :32], "seq", opposite)
    slot = jnp.where(place[0] == 0, grad[:, 32:40], grad[:, :8])
    slot = lax.ppermute(slot, "seq", heads_to)
    mid = lax.all_to_all(back.reshape(SEQ, ROWS, HALF), "seq", 0, 0, tiled=True)
    grad = pl.pallas_call(
        kernel_g,
        in_specs=[SMEM] + [VMEM] * 6,
        out_specs=VMEM,
        out_shape=jax.ShapeDtypeStruct((2, 64, N), BF),
        scratch_shapes=[pltpu.VMEM((2, 112, N), BF)],
        compiler_params=PARAMS,
        cost_estimate=pl.CostEstimate(flops=100000000, bytes_accessed=1000000, transcendentals=0),
    )(place, grad, far, slot, g_own, g_mirror, flip)
    for bit in (2, 4, 1):
        other = lax.ppermute(grad, "dp", [(d, d ^ bit) for d in range(8)])
        grad = (grad.astype(F32) + other.astype(F32)).astype(BF)
    output, grad_signal = pl.pallas_call(
        kernel_c,
        in_specs=[SMEM, VMEM, VMEM],
        out_specs=[VMEM, VMEM],
        out_shape=[jax.ShapeDtypeStruct((128, N), BF)] * 2,
        scratch_shapes=[
            pltpu.VMEM((2, N, 128), F32),
            pltpu.VMEM((2, 256, 128), F32),
            pltpu.VMEM((2, 256, 128), F32),
        ],
        compiler_params=PARAMS,
        cost_estimate=pl.CostEstimate(flops=400000000, bytes_accessed=2000000, transcendentals=0),
    )(place, mid.reshape(N, HALF), table)
    return output.reshape(shape), grad_signal.reshape(shape), grad.reshape(2, 8, 8, N)


def solution(mesh):
    placed = (P(None, "dp", "seq", None), P(None, "dp", "seq", None), P(None, None, "seq", None))
    return jax.shard_map(body, mesh=mesh, in_specs=placed, out_specs=placed, check_vma=False)
```

```python
import math

import jax
import jax.numpy as jnp
import numpy as np
from jax import lax
from jax.experimental import pallas as pl
from jax.experimental.pallas import tpu as pltpu
from jax.sharding import PartitionSpec as P

N = 512
SEQ = 64
ROWS = N // SEQ
HALF = N // 2
BF = jnp.bfloat16
F32 = jnp.float32
VMEM = pl.BlockSpec(memory_space=pltpu.VMEM)
SMEM = pl.BlockSpec(memory_space=pltpu.SMEM)
PARAMS = pltpu.CompilerParams(vmem_limit_bytes=20 * 2**20)

LAST = 31


def unit_tables():
    steps = np.arange(N, dtype=np.int32)
    phases = (steps[:, None] * steps[None, :] % N).astype(np.float32) * np.float32(
        2.0 * math.pi / N
    )
    factor = np.float32(1.0 / math.sqrt(N))
    return (np.cos(phases) * factor).astype(BF), (-np.sin(phases) * factor).astype(BF)


def first_table():
    cos_t, sin_t = unit_tables()
    col = np.arange(HALF)
    place = col % 64
    slot = 2 * (col // 128) + col // 64 % 2
    row = 8 * place + slot + np.where(place >= 32, 1, 8 * (slot == 0))
    re, im = cos_t[:, row], sin_t[:, row]
    im[:, LAST] = cos_t[:, 0]
    return np.concatenate([re, im], axis=1)


def lanes():
    lane = np.arange(HALF)
    slot = 2 * (lane // 32 % 2) + lane // 128
    return slot, lane // 64 % 2, lane // 16 % 2, lane // 2 % 8, lane % 2


def filter_selectors():
    slot, _, _, filt, chan = lanes()
    own = np.zeros((3, 112, HALF), np.float32)
    mirror = np.zeros((3, 112, HALF), np.float32)
    for lane in range(HALF):
        k, f = slot[lane], filt[lane]
        for kind in (0, 1):
            own[kind, f * 8 + k if k else 96 + f, lane] = 0.5
            mirror[kind, 64 + f * 4 + (4 - k) % 4, lane] = 0.5
        own[2, f * 8 + k + 1, lane] = 0.5
        mirror[2, 64 + f * 4 + 3 - k, lane] = 0.5
        if k == 0:
            own[0, :, lane] = 0
            mirror[0, :, lane] = 0
            source = 96 + f if chan[lane] else 64 + f * 4
            own[0, source, lane] = 0.5
            mirror[0, source, lane] = 0.5
    return own.astype(BF), mirror.astype(BF)


def gather_tables():
    slot, part, kind, filt, chan = lanes()
    out = np.zeros((2, 2, 48, HALF), np.float32)
    for lane in range(HALF):
        if kind[lane]:
            continue
        for first in range(2):
            for ri in range(2):
                sign = -1.0 if ri and part[lane] else 1.0
                extra = slot[lane] == 0 and chan[lane] == 1
                if not (first and extra):
                    out[first, ri, slot[lane] * 8 + filt[lane], lane] = sign
                if extra:
                    out[first, ri, 32 + filt[lane], lane] = sign
    return out.astype(BF)


def grad_selectors():
    own = np.zeros((4, 64, 112), np.float32)
    mirror = np.zeros((4, 64, 112), np.float32)
    for f in range(8):
        for row in range(8):
            at = f * 8 + row
            for kind in (0, 1):
                if row < 4:
                    own[kind, at, row * 8 + f if row else 96 + f] = 1
                else:
                    mirror[kind, at, 48 + (7 - row) * 8 + f] = 1
            for kind in (2, 3):
                if 0 < row < 5:
                    own[kind, at, (row - 1) * 8 + f] = 1
                else:
                    mirror[kind, at, 48 + (8 - row) % 8 * 8 + f] = 1
        own[0, f * 8, 96 + f] = 0.5
        mirror[0, f * 8, 96 + f] = 0.5
        own[3, f * 8, 48 + f] = 0.5
        mirror[3, f * 8, 48 + f] = 0.5
    return own.astype(BF), mirror.astype(BF)


def payload_selectors():
    tail = np.zeros((2, 32, 64), np.float32)
    head = np.zeros((8, 64), np.float32)
    for f in range(8):
        head[f, f * 8] = 1
        for row in range(4):
            tail[0, f * 4 + row, f * 8 + 4 + row] = 1
            tail[1, f * 4 + row, f * 8 + (4 + row if row else 0)] = 1
    return tail.astype(BF), head.astype(BF)


def dot(a, b, dims=((1,), (0,)), precision=None):
    return lax.dot_general(a, b, (dims, ((), ())), precision=precision, preferred_element_type=F32)


def turn(idx_ref, chan):
    shape = (ROWS, HALF)
    lane = lax.broadcasted_iota(jnp.int32, shape, 1)
    row = idx_ref[0] * ROWS + lax.broadcasted_iota(jnp.int32, shape, 0)
    place = lane & 63
    slot = 2 * (lane >> 7) + ((lane >> 6) & 1)
    col = 8 * place + slot + jnp.where(place >= 32, 1, jnp.where(slot == 0, 8, 0))
    if chan:
        col = jnp.where(lane == LAST, 0, col)
    phases = (row * col).astype(F32) * (-2.0 * math.pi / (N * N))
    return jnp.cos(phases), jnp.sin(phases)


def swap_first(re, im):
    first = lax.broadcasted_iota(jnp.int32, re[0].shape, 2) == LAST
    return (re[0], jnp.where(first, im[0], re[1])), (jnp.where(first, re[1], im[0]), im[1])


def kernel_a(idx_ref, sig_ref, cot_ref, t_ref, f_ref, tail_ref, head_ref, out_ref, tails_ref,
             heads_ref, yre, yim, z):
    upper = idx_ref[0] >> 5
    for ri in range(2):
        tails_ref[ri] = dot(tail_ref[upper], f_ref[ri]).astype(BF)
        heads_ref[ri] = dot(head_ref[...], f_ref[ri]).astype(BF)
    turns = [turn(idx_ref, chan) for chan in range(2)]
    for half, ref in enumerate((sig_ref, cot_ref)):
        x = ref[...]
        re = dot(x, t_ref[:, :HALF]).reshape(8, 2, ROWS, HALF)
        im = dot(x, t_ref[:, HALF:]).reshape(8, 2, ROWS, HALF)
        re, im = swap_first((re[:, 0], re[:, 1]), (im[:, 0], im[:, 1]))
        at = pl.ds(half * 128, 128)
        out_re = [re[c] * turns[c][0] - im[c] * turns[c][1] for c in range(2)]
        out_im = [re[c] * turns[c][1] + im[c] * turns[c][0] for c in range(2)]
        for y, v in ((yre, out_re), (yim, out_im)):
            v = jnp.stack(v, axis=1).reshape(128, HALF)
            for s in range(2):
                y[s, at, :] = v[:, s * 128 : (s + 1) * 128]
    for r in range(ROWS):
        rows = [y[s, pl.ds(r, 32, stride=ROWS), :] for y in (yre, yim) for s in range(2)]
        block = jnp.concatenate(rows, axis=0).T
        for p in range(2):
            z[p, pl.ds(r, 64, stride=ROWS), :] = block[p * 64 : (p + 1) * 64]
    for p in range(2):
        out_ref[:, p * 128 : (p + 1) * 128] = z[p].astype(BF)


def kernel_f(idx_ref, f_ref, tail_ref, head_ref, own_ref, mirror_ref, flip_ref, h_ref, rows):
    place = idx_ref[0]
    kind = jnp.where(place == LAST, 0, jnp.where(place < 32, 1, 2))
    rows[:, :64, :] = f_ref[...]
    rows[:, 64:96, :] = tail_ref[...]
    rows[:, 96:, :] = jnp.zeros((2, 16, N), BF)
    rows[:, 96:104, :] = head_ref[...]
    lane = lax.broadcasted_iota(jnp.int32, (N, HALF), 1)
    shifted = ((lane & ~30) == 1) | ((lane & ~30) == 65)
    shifted = shifted & (place == LAST)
    negative = ((lane >> 6) & 1) == ((lane >> 4) & 1)
    for ri in range(2):
        near = dot(rows[ri], own_ref[kind], ((0,), (0,)))
        far = dot(rows[ri], mirror_ref[kind], ((0,), (0,))).astype(BF)
        far = dot(flip_ref[...], far)
        far = jnp.where(shifted, pltpu.roll(far, 1, 0), far)
        if ri == 0:
            h_ref[:, :HALF] = near + far
        else:
            value = near - far
            h_ref[:, HALF:] = jnp.where(negative, -value, value)


def kernel_b(idx_ref, r_ref, wc_ref, ws_ref, h_ref, gather_ref, v_ref, g_ref, prod):
    first = jnp.where(idx_ref[0] == LAST, 1, 0)
    sign = jnp.where(lax.broadcasted_iota(jnp.int32, (128, 128), 1) < 64, -1.0, 1.0)
    for k in range(4):
        at = pl.ds(k * 128, 128)
        p1 = dot(wc_ref[at, :], r_ref[...])
        p2 = dot(ws_ref[at, :], r_ref[...])
        pairs = []
        for p in range(2):
            cols = slice(p * 128, (p + 1) * 128)
            x = p1[:, cols] + sign * pltpu.roll(p2[:, cols], 64, 1)
            swapped = pltpu.roll(x, 64, 1)
            h1 = h_ref[at, p * 128 : (p + 1) * 128]
            h2 = h_ref[at, HALF + p * 128 : HALF + (p + 1) * 128]
            prod[at, cols] = (h1 * x + h2 * swapped).astype(BF)
            pairs.append((pltpu.roll(x, 112, 1) * x, pltpu.roll(x, 48, 1) * x))
        for ri in range(2):
            terms = jnp.concatenate([pairs[0][ri], pairs[1][ri]], axis=1)
            high = terms.astype(BF)
            low = (terms - high.astype(F32)).astype(BF)
            take = gather_ref[first, ri]
            total = dot(take, high, ((1,), (1,))) + dot(take, low, ((1,), (1,)))
            g_ref[ri, :, at] = total.astype(BF)
    for k in range(4):
        at = pl.ds(k * 128, 128)
        q1 = dot(wc_ref[at, :], prod[...])
        q2 = dot(ws_ref[at, :], prod[...])
        for p in range(2):
            cols = slice(p * 128, (p + 1) * 128)
            v_ref[at, cols] = (q1[:, cols] - sign * pltpu.roll(q2[:, cols], 64, 1)).astype(BF)


def kernel_c(idx_ref, v_ref, t_ref, out_ref, grad_ref, z, yre, yim):
    for p in range(2):
        z[p] = v_ref[:, p * 128 : (p + 1) * 128].astype(F32)
    for r in range(ROWS):
        rows = [z[p, pl.ds(r, 64, stride=ROWS), :] for p in range(2)]
        block = jnp.concatenate(rows, axis=0).T
        for ri, y in enumerate((yre, yim)):
            for s in range(2):
                at = ri * 64 + s * 32
                y[s, pl.ds(r, 32, stride=ROWS), :] = block[at : at + 32]
    double = jnp.where(lax.broadcasted_iota(jnp.int32, (ROWS, HALF), 1) == LAST, 1.0, 2.0)
    turns = [[t * double for t in turn(idx_ref, chan)] for chan in range(2)]
    for half, ref in enumerate((out_ref, grad_ref)):
        at = pl.ds(half * 128, 128)
        re, im = (
            jnp.concatenate([y[s, at, :] for s in range(2)], axis=1).reshape(8, 2, ROWS, HALF)
            for y in (yre, yim)
        )
        mid_re = [re[:, c] * turns[c][0] + im[:, c] * turns[c][1] for c in range(2)]
        mid_im = [im[:, c] * turns[c][0] - re[:, c] * turns[c][1] for c in range(2)]
        mid_re, mid_im = (
            jnp.stack(v, axis=1).reshape(128, HALF).astype(BF) for v in swap_first(mid_re, mid_im)
        )
        total = dot(mid_re, t_ref[:, :HALF], ((1,), (1,)))
        total = total + dot(mid_im, t_ref[:, HALF:], ((1,), (1,)))
        ref[...] = total.astype(BF)


def kernel_g(idx_ref, g_ref, far_ref, head_ref, own_ref, mirror_ref, flip_ref, out_ref, rows):
    place = idx_ref[0]
    kind = jnp.where(
        place == 0, 0, jnp.where(place == 32, 3, jnp.where(place < 32, 1, 2))
    )
    rows[:, :48, :] = g_ref[...]
    rows[:, 48:80, :] = far_ref[...]
    rows[:, 80:96, :] = jnp.zeros((2, 16, N), BF)
    rows[:, 96:, :] = jnp.zeros((2, 16, N), BF)
    rows[:, 96:104, :] = head_ref[...]
    row = lax.broadcasted_iota(jnp.int32, (64, N), 0)
    shifted = ((row & 7) == 0) & (place == 0)
    for ri in range(2):
        near = dot(own_ref[kind], rows[ri])
        far = dot(mirror_ref[kind], rows[ri]).astype(BF)
        far = dot(far, flip_ref[...])
        far = jnp.where(shifted, pltpu.roll(far, 1, 1), far)
        out_ref[ri] = (near + far if ri == 0 else near - far).astype(BF)


def body(signal, cotangent, filter_spec):
    shape = signal.shape
    place = lax.axis_index("seq").astype(jnp.int32).reshape(1)
    table = jnp.asarray(first_table())
    cos_t, sin_t = (jnp.asarray(t) for t in unit_tables())
    flip = jnp.asarray(np.eye(N, dtype=np.float32)[::-1].astype(BF))
    tail, head = (jnp.asarray(t) for t in payload_selectors())
    f_own, f_mirror = (jnp.asarray(t) for t in filter_selectors())
    g_own, g_mirror = (jnp.asarray(t) for t in grad_selectors())
    gather = jnp.asarray(gather_tables())
    opposite = [(d, SEQ - 1 - d) for d in range(SEQ)]
    down = [(d, d // 32 * 32 + (d - 1) % 32) for d in range(SEQ)]
    up = [(b, a) for a, b in down]
    filt = filter_spec.reshape(2, 64, N)
    sent, tails, heads = pl.pallas_call(
        kernel_a,
        in_specs=[SMEM] + [VMEM] * 6,
        out_specs=[VMEM] * 3,
        out_shape=[
            jax.ShapeDtypeStruct((N, HALF), BF),
            jax.ShapeDtypeStruct((2, 32, N), BF),
            jax.ShapeDtypeStruct((2, 8, N), BF),
        ],
        scratch_shapes=[
            pltpu.VMEM((2, 256, 128), F32),
            pltpu.VMEM((2, 256, 128), F32),
            pltpu.VMEM((2, N, 128), F32),
        ],
    )(place, signal.reshape(128, N), cotangent.reshape(128, N), table, filt, tail, head)
    got = lax.all_to_all(sent.reshape(SEQ, ROWS, HALF), "seq", 0, 0, tiled=True)
    tails = lax.ppermute(tails, "seq", opposite)
    heads = lax.ppermute(heads, "seq", down)
    spread = pl.pallas_call(
        kernel_f,
        in_specs=[SMEM] + [VMEM] * 6,
        out_specs=VMEM,
        out_shape=jax.ShapeDtypeStruct((N, N), F32),
        scratch_shapes=[pltpu.VMEM((2, 112, N), BF)],
        compiler_params=PARAMS,
        cost_estimate=pl.CostEstimate(flops=400000000, bytes_accessed=2000000, transcendentals=0),
    )(place, filt, tails, heads, f_own, f_mirror, flip)
    back, grad = pl.pallas_call(
        kernel_b,
        in_specs=[SMEM] + [VMEM] * 5,
        out_specs=[VMEM, VMEM],
        out_shape=[
            jax.ShapeDtypeStruct((N, HALF), BF),
            jax.ShapeDtypeStruct((2, 48, N), BF),
        ],
        scratch_shapes=[pltpu.VMEM((N, HALF), BF)],
        compiler_params=PARAMS,
    )(place, got.reshape(N, HALF), cos_t, sin_t, spread, gather)
    far = lax.ppermute(grad[:, :32], "seq", opposite)
    slot = jnp.where(place[0] == LAST, grad[:, 32:40], grad[:, :8])
    slot = lax.ppermute(slot, "seq", up)
    mid = lax.all_to_all(back.reshape(SEQ, ROWS, HALF), "seq", 0, 0, tiled=True)
    grad = pl.pallas_call(
        kernel_g,
        in_specs=[SMEM] + [VMEM] * 6,
        out_specs=VMEM,
        out_shape=jax.ShapeDtypeStruct((2, 64, N), BF),
        scratch_shapes=[pltpu.VMEM((2, 112, N), BF)],
        compiler_params=PARAMS,
        cost_estimate=pl.CostEstimate(flops=100000000, bytes_accessed=1000000, transcendentals=0),
    )(place, grad, far, slot, g_own, g_mirror, flip)
    for bit in (2, 4, 1):
        other = lax.ppermute(grad, "dp", [(d, d ^ bit) for d in range(8)])
        grad = (grad.astype(F32) + other.astype(F32)).astype(BF)
    output, grad_signal = pl.pallas_call(
        kernel_c,
        in_specs=[SMEM, VMEM, VMEM],
        out_specs=[VMEM, VMEM],
        out_shape=[jax.ShapeDtypeStruct((128, N), BF)] * 2,
        scratch_shapes=[
            pltpu.VMEM((2, N, 128), F32),
            pltpu.VMEM((2, 256, 128), F32),
            pltpu.VMEM((2, 256, 128), F32),
        ],
        compiler_params=PARAMS,
        cost_estimate=pl.CostEstimate(flops=400000000, bytes_accessed=2000000, transcendentals=0),
    )(place, mid.reshape(N, HALF), table)
    return output.reshape(shape), grad_signal.reshape(shape), grad.reshape(2, 8, 8, N)


def solution(mesh):
    placed = (P(None, "dp", "seq", None), P(None, "dp", "seq", None), P(None, None, "seq", None))
    return jax.shard_map(body, mesh=mesh, in_specs=placed, out_specs=placed, check_vma=False)
```

```python
import math

import jax
import jax.numpy as jnp
import numpy as np
from jax import lax
from jax.experimental import pallas as pl
from jax.experimental.pallas import tpu as pltpu
from jax.sharding import PartitionSpec as P

N = 512
SEQ = 64
ROWS = N // SEQ
HALF = N // 2
BF = jnp.bfloat16
F32 = jnp.float32
VMEM = pl.BlockSpec(memory_space=pltpu.VMEM)
SMEM = pl.BlockSpec(memory_space=pltpu.SMEM)
PARAMS = pltpu.CompilerParams(vmem_limit_bytes=20 * 2**20)

LAST = 31


def unit_tables():
    steps = np.arange(N, dtype=np.int32)
    phases = (steps[:, None] * steps[None, :] % N).astype(np.float32) * np.float32(
        2.0 * math.pi / N
    )
    factor = np.float32(1.0 / math.sqrt(N))
    return (np.cos(phases) * factor).astype(BF), (-np.sin(phases) * factor).astype(BF)


def first_table():
    cos_t, sin_t = unit_tables()
    col = np.arange(HALF)
    place = col % 64
    slot = 2 * (col // 128) + col // 64 % 2
    row = 8 * place + slot + np.where(place >= 32, 1, 8 * (slot == 0))
    re, im = cos_t[:, row], sin_t[:, row]
    im[:, LAST] = cos_t[:, 0]
    return np.concatenate([re, im], axis=1)


def lanes():
    lane = np.arange(HALF)
    slot = 2 * (lane // 32 % 2) + lane // 128
    return slot, lane // 64 % 2, lane // 16 % 2, lane // 2 % 8, lane % 2


def filter_selectors():
    slot, _, _, filt, chan = lanes()
    own = np.zeros((3, 112, HALF), np.float32)
    mirror = np.zeros((3, 112, HALF), np.float32)
    for lane in range(HALF):
        k, f = slot[lane], filt[lane]
        for kind in (0, 1):
            own[kind, f * 8 + k if k else 96 + f, lane] = 0.5
            mirror[kind, 64 + f * 4 + (4 - k) % 4, lane] = 0.5
        own[2, f * 8 + k + 1, lane] = 0.5
        mirror[2, 64 + f * 4 + 3 - k, lane] = 0.5
        if k == 0:
            own[0, :, lane] = 0
            mirror[0, :, lane] = 0
            source = 96 + f if chan[lane] else 64 + f * 4
            own[0, source, lane] = 0.5
            mirror[0, source, lane] = 0.5
    return own.astype(BF), mirror.astype(BF)


def gather_tables():
    slot, part, kind, filt, chan = lanes()
    out = np.zeros((2, 2, 48, HALF), np.float32)
    for lane in range(HALF):
        if kind[lane]:
            continue
        for first in range(2):
            for ri in range(2):
                sign = -1.0 if ri and part[lane] else 1.0
                extra = slot[lane] == 0 and chan[lane] == 1
                if not (first and extra):
                    out[first, ri, slot[lane] * 8 + filt[lane], lane] = sign
                if extra:
                    out[first, ri, 32 + filt[lane], lane] = sign
    return out.astype(BF)


def grad_selectors():
    own = np.zeros((4, 64, 112), np.float32)
    mirror = np.zeros((4, 64, 112), np.float32)
    for f in range(8):
        for row in range(8):
            at = f * 8 + row
            for kind in (0, 1):
                if row < 4:
                    own[kind, at, row * 8 + f if row else 96 + f] = 1
                else:
                    mirror[kind, at, 48 + (7 - row) * 8 + f] = 1
            for kind in (2, 3):
                if 0 < row < 5:
                    own[kind, at, (row - 1) * 8 + f] = 1
                else:
                    mirror[kind, at, 48 + (8 - row) % 8 * 8 + f] = 1
        own[0, f * 8, 96 + f] = 0.5
        mirror[0, f * 8, 96 + f] = 0.5
        own[3, f * 8, 48 + f] = 0.5
        mirror[3, f * 8, 48 + f] = 0.5
    return own.astype(BF), mirror.astype(BF)


def payload_selectors():
    tail = np.zeros((2, 32, 64), np.float32)
    head = np.zeros((8, 64), np.float32)
    for f in range(8):
        head[f, f * 8] = 1
        for row in range(4):
            tail[0, f * 4 + row, f * 8 + 4 + row] = 1
            tail[1, f * 4 + row, f * 8 + (4 + row if row else 0)] = 1
    return tail.astype(BF), head.astype(BF)


def dot(a, b, dims=((1,), (0,)), precision=None):
    return lax.dot_general(a, b, (dims, ((), ())), precision=precision, preferred_element_type=F32)


def turn(idx_ref, chan):
    shape = (ROWS, HALF)
    lane = lax.broadcasted_iota(jnp.int32, shape, 1)
    row = idx_ref[0] * ROWS + lax.broadcasted_iota(jnp.int32, shape, 0)
    place = lane & 63
    slot = 2 * (lane >> 7) + ((lane >> 6) & 1)
    col = 8 * place + slot + jnp.where(place >= 32, 1, jnp.where(slot == 0, 8, 0))
    if chan:
        col = jnp.where(lane == LAST, 0, col)
    phases = (row * col).astype(F32) * (-2.0 * math.pi / (N * N))
    return jnp.cos(phases), jnp.sin(phases)


def swap_first(re, im):
    first = lax.broadcasted_iota(jnp.int32, re[0].shape, 2) == LAST
    return (re[0], jnp.where(first, im[0], re[1])), (jnp.where(first, re[1], im[0]), im[1])


def kernel_a(idx_ref, sig_ref, cot_ref, t_ref, f_ref, tail_ref, head_ref, out_ref, tails_ref,
             heads_ref, yre, yim, z):
    upper = idx_ref[0] >> 5
    for ri in range(2):
        tails_ref[ri] = dot(tail_ref[upper], f_ref[ri]).astype(BF)
        heads_ref[ri] = dot(head_ref[...], f_ref[ri]).astype(BF)
    turns = [turn(idx_ref, chan) for chan in range(2)]
    both = dot(jnp.concatenate([sig_ref[...], cot_ref[...]], axis=0), t_ref[...])
    for half in range(2):
        part = both[half * 128 : (half + 1) * 128]
        re = part[:, :HALF].reshape(8, 2, ROWS, HALF)
        im = part[:, HALF:].reshape(8, 2, ROWS, HALF)
        re, im = swap_first((re[:, 0], re[:, 1]), (im[:, 0], im[:, 1]))
        at = pl.ds(half * 128, 128)
        out_re = [re[c] * turns[c][0] - im[c] * turns[c][1] for c in range(2)]
        out_im = [re[c] * turns[c][1] + im[c] * turns[c][0] for c in range(2)]
        for y, v in ((yre, out_re), (yim, out_im)):
            v = jnp.stack(v, axis=1).reshape(128, HALF)
            for s in range(2):
                y[s, at, :] = v[:, s * 128 : (s + 1) * 128]
    for r in range(ROWS):
        rows = [y[s, pl.ds(r, 32, stride=ROWS), :] for y in (yre, yim) for s in range(2)]
        block = jnp.concatenate(rows, axis=0).T
        for p in range(2):
            z[p, pl.ds(r, 64, stride=ROWS), :] = block[p * 64 : (p + 1) * 64]
    for p in range(2):
        out_ref[:, p * 128 : (p + 1) * 128] = z[p].astype(BF)


def kernel_f(idx_ref, f_ref, tail_ref, head_ref, own_ref, mirror_ref, flip_ref, h_ref, rows):
    place = idx_ref[0]
    kind = jnp.where(place == LAST, 0, jnp.where(place < 32, 1, 2))
    rows[:, :64, :] = f_ref[...]
    rows[:, 64:96, :] = tail_ref[...]
    rows[:, 96:, :] = jnp.zeros((2, 16, N), BF)
    rows[:, 96:104, :] = head_ref[...]
    lane = lax.broadcasted_iota(jnp.int32, (N, HALF), 1)
    shifted = ((lane & ~30) == 1) | ((lane & ~30) == 65)
    shifted = shifted & (place == LAST)
    negative = ((lane >> 6) & 1) == ((lane >> 4) & 1)
    for ri in range(2):
        near = dot(rows[ri], own_ref[kind], ((0,), (0,)))
        far = dot(rows[ri], mirror_ref[kind], ((0,), (0,))).astype(BF)
        far = dot(flip_ref[...], far)
        far = jnp.where(shifted, pltpu.roll(far, 1, 0), far)
        if ri == 0:
            h_ref[:, :HALF] = near + far
        else:
            value = near - far
            h_ref[:, HALF:] = jnp.where(negative, -value, value)


def kernel_b(idx_ref, r_ref, wc_ref, ws_ref, h_ref, gather_ref, v_ref, g_ref, prod):
    first = jnp.where(idx_ref[0] == LAST, 1, 0)
    sign = jnp.where(lax.broadcasted_iota(jnp.int32, (N, 128), 1) < 64, -1.0, 1.0)
    p1 = dot(wc_ref[...], r_ref[...])
    p2 = dot(ws_ref[...], r_ref[...])
    pairs = []
    for p in range(2):
        cols = slice(p * 128, (p + 1) * 128)
        x = p1[:, cols] + sign * pltpu.roll(p2[:, cols], 64, 1)
        swapped = pltpu.roll(x, 64, 1)
        h1 = h_ref[:, p * 128 : (p + 1) * 128]
        h2 = h_ref[:, HALF + p * 128 : HALF + (p + 1) * 128]
        prod[:, cols] = (h1 * x + h2 * swapped).astype(BF)
        pairs.append((pltpu.roll(x, 112, 1) * x, pltpu.roll(x, 48, 1) * x))
    for ri in range(2):
        terms = jnp.concatenate([pairs[0][ri], pairs[1][ri]], axis=1)
        high = terms.astype(BF)
        low = (terms - high.astype(F32)).astype(BF)
        take = gather_ref[first, ri]
        total = dot(take, high, ((1,), (1,))) + dot(take, low, ((1,), (1,)))
        g_ref[ri] = total.astype(BF)
    q1 = dot(wc_ref[...], prod[...])
    q2 = dot(ws_ref[...], prod[...])
    for p in range(2):
        cols = slice(p * 128, (p + 1) * 128)
        v_ref[:, cols] = (q1[:, cols] - sign * pltpu.roll(q2[:, cols], 64, 1)).astype(BF)


def kernel_c(idx_ref, v_ref, t_ref, out_ref, grad_ref, z, yre, yim):
    for p in range(2):
        z[p] = v_ref[:, p * 128 : (p + 1) * 128].astype(F32)
    for r in range(ROWS):
        rows = [z[p, pl.ds(r, 64, stride=ROWS), :] for p in range(2)]
        block = jnp.concatenate(rows, axis=0).T
        for ri, y in enumerate((yre, yim)):
            for s in range(2):
                at = ri * 64 + s * 32
                y[s, pl.ds(r, 32, stride=ROWS), :] = block[at : at + 32]
    double = jnp.where(lax.broadcasted_iota(jnp.int32, (ROWS, HALF), 1) == LAST, 1.0, 2.0)
    turns = [[t * double for t in turn(idx_ref, chan)] for chan in range(2)]
    for half, ref in enumerate((out_ref, grad_ref)):
        at = pl.ds(half * 128, 128)
        re, im = (
            jnp.concatenate([y[s, at, :] for s in range(2)], axis=1).reshape(8, 2, ROWS, HALF)
            for y in (yre, yim)
        )
        mid_re = [re[:, c] * turns[c][0] + im[:, c] * turns[c][1] for c in range(2)]
        mid_im = [im[:, c] * turns[c][0] - re[:, c] * turns[c][1] for c in range(2)]
        mid_re, mid_im = (
            jnp.stack(v, axis=1).reshape(128, HALF).astype(BF) for v in swap_first(mid_re, mid_im)
        )
        total = dot(mid_re, t_ref[:, :HALF], ((1,), (1,)))
        total = total + dot(mid_im, t_ref[:, HALF:], ((1,), (1,)))
        ref[...] = total.astype(BF)


def kernel_g(idx_ref, g_ref, far_ref, head_ref, own_ref, mirror_ref, flip_ref, out_ref, rows):
    place = idx_ref[0]
    kind = jnp.where(
        place == 0, 0, jnp.where(place == 32, 3, jnp.where(place < 32, 1, 2))
    )
    rows[:, :48, :] = g_ref[...]
    rows[:, 48:80, :] = far_ref[...]
    rows[:, 80:96, :] = jnp.zeros((2, 16, N), BF)
    rows[:, 96:, :] = jnp.zeros((2, 16, N), BF)
    rows[:, 96:104, :] = head_ref[...]
    row = lax.broadcasted_iota(jnp.int32, (64, N), 0)
    shifted = ((row & 7) == 0) & (place == 0)
    for ri in range(2):
        near = dot(own_ref[kind], rows[ri])
        far = dot(mirror_ref[kind], rows[ri]).astype(BF)
        far = dot(far, flip_ref[...])
        far = jnp.where(shifted, pltpu.roll(far, 1, 1), far)
        out_ref[ri] = (near + far if ri == 0 else near - far).astype(BF)


def body(signal, cotangent, filter_spec):
    shape = signal.shape
    place = lax.axis_index("seq").astype(jnp.int32).reshape(1)
    table = jnp.asarray(first_table())
    cos_t, sin_t = (jnp.asarray(t) for t in unit_tables())
    flip = jnp.asarray(np.eye(N, dtype=np.float32)[::-1].astype(BF))
    tail, head = (jnp.asarray(t) for t in payload_selectors())
    f_own, f_mirror = (jnp.asarray(t) for t in filter_selectors())
    g_own, g_mirror = (jnp.asarray(t) for t in grad_selectors())
    gather = jnp.asarray(gather_tables())
    opposite = [(d, SEQ - 1 - d) for d in range(SEQ)]
    down = [(d, d // 32 * 32 + (d - 1) % 32) for d in range(SEQ)]
    up = [(b, a) for a, b in down]
    filt = filter_spec.reshape(2, 64, N)
    sent, tails, heads = pl.pallas_call(
        kernel_a,
        in_specs=[SMEM] + [VMEM] * 6,
        out_specs=[VMEM] * 3,
        out_shape=[
            jax.ShapeDtypeStruct((N, HALF), BF),
            jax.ShapeDtypeStruct((2, 32, N), BF),
            jax.ShapeDtypeStruct((2, 8, N), BF),
        ],
        scratch_shapes=[
            pltpu.VMEM((2, 256, 128), F32),
            pltpu.VMEM((2, 256, 128), F32),
            pltpu.VMEM((2, N, 128), F32),
        ],
    )(place, signal.reshape(128, N), cotangent.reshape(128, N), table, filt, tail, head)
    got = lax.all_to_all(sent.reshape(SEQ, ROWS, HALF), "seq", 0, 0, tiled=True)
    tails = lax.ppermute(tails, "seq", opposite)
    heads = lax.ppermute(heads, "seq", down)
    spread = pl.pallas_call(
        kernel_f,
        in_specs=[SMEM] + [VMEM] * 6,
        out_specs=VMEM,
        out_shape=jax.ShapeDtypeStruct((N, N), F32),
        scratch_shapes=[pltpu.VMEM((2, 112, N), BF)],
        compiler_params=PARAMS,
        cost_estimate=pl.CostEstimate(flops=400000000, bytes_accessed=2000000, transcendentals=0),
    )(place, filt, tails, heads, f_own, f_mirror, flip)
    back, grad = pl.pallas_call(
        kernel_b,
        in_specs=[SMEM] + [VMEM] * 5,
        out_specs=[VMEM, VMEM],
        out_shape=[
            jax.ShapeDtypeStruct((N, HALF), BF),
            jax.ShapeDtypeStruct((2, 48, N), BF),
        ],
        scratch_shapes=[pltpu.VMEM((N, HALF), BF)],
        compiler_params=PARAMS,
    )(place, got.reshape(N, HALF), cos_t, sin_t, spread, gather)
    far = lax.ppermute(grad[:, :32], "seq", opposite)
    slot = jnp.where(place[0] == LAST, grad[:, 32:40], grad[:, :8])
    slot = lax.ppermute(slot, "seq", up)
    mid = lax.all_to_all(back.reshape(SEQ, ROWS, HALF), "seq", 0, 0, tiled=True)
    grad = pl.pallas_call(
        kernel_g,
        in_specs=[SMEM] + [VMEM] * 6,
        out_specs=VMEM,
        out_shape=jax.ShapeDtypeStruct((2, 64, N), BF),
        scratch_shapes=[pltpu.VMEM((2, 112, N), BF)],
        compiler_params=PARAMS,
        cost_estimate=pl.CostEstimate(flops=100000000, bytes_accessed=1000000, transcendentals=0),
    )(place, grad, far, slot, g_own, g_mirror, flip)
    for bit in (2, 4, 1):
        other = lax.ppermute(grad, "dp", [(d, d ^ bit) for d in range(8)])
        grad = (grad.astype(F32) + other.astype(F32)).astype(BF)
    output, grad_signal = pl.pallas_call(
        kernel_c,
        in_specs=[SMEM, VMEM, VMEM],
        out_specs=[VMEM, VMEM],
        out_shape=[jax.ShapeDtypeStruct((128, N), BF)] * 2,
        scratch_shapes=[
            pltpu.VMEM((2, N, 128), F32),
            pltpu.VMEM((2, 256, 128), F32),
            pltpu.VMEM((2, 256, 128), F32),
        ],
        compiler_params=PARAMS,
        cost_estimate=pl.CostEstimate(flops=400000000, bytes_accessed=2000000, transcendentals=0),
    )(place, mid.reshape(N, HALF), table)
    return output.reshape(shape), grad_signal.reshape(shape), grad.reshape(2, 8, 8, N)


def solution(mesh):
    placed = (P(None, "dp", "seq", None), P(None, "dp", "seq", None), P(None, None, "seq", None))
    return jax.shard_map(body, mesh=mesh, in_specs=placed, out_specs=placed, check_vma=False)
```

```python
import math

import jax
import jax.numpy as jnp
import numpy as np
from jax import lax
from jax.experimental import pallas as pl
from jax.experimental.pallas import tpu as pltpu
from jax.sharding import PartitionSpec as P

N = 512
SEQ = 64
ROWS = N // SEQ
HALF = N // 2
BF = jnp.bfloat16
F32 = jnp.float32
VMEM = pl.BlockSpec(memory_space=pltpu.VMEM)
SMEM = pl.BlockSpec(memory_space=pltpu.SMEM)
PARAMS = pltpu.CompilerParams(vmem_limit_bytes=20 * 2**20)

LAST = 31


def unit_tables():
    steps = np.arange(N, dtype=np.int32)
    phases = (steps[:, None] * steps[None, :] % N).astype(np.float32) * np.float32(
        2.0 * math.pi / N
    )
    factor = np.float32(1.0 / math.sqrt(N))
    return (np.cos(phases) * factor).astype(BF), (-np.sin(phases) * factor).astype(BF)


def first_table():
    cos_t, sin_t = unit_tables()
    col = np.arange(HALF)
    place = col % 64
    slot = 2 * (col // 128) + col // 64 % 2
    row = 8 * place + slot + np.where(place >= 32, 1, 8 * (slot == 0))
    re, im = cos_t[:, row], sin_t[:, row]
    im[:, LAST] = cos_t[:, 0]
    return np.concatenate([re, im], axis=1)


def lanes():
    lane = np.arange(HALF)
    slot = 2 * (lane // 32 % 2) + lane // 128
    return slot, lane // 64 % 2, lane // 16 % 2, lane // 2 % 8, lane % 2


def filter_selectors():
    slot, _, _, filt, chan = lanes()
    own = np.zeros((3, 112, HALF), np.float32)
    mirror = np.zeros((3, 112, HALF), np.float32)
    for lane in range(HALF):
        k, f = slot[lane], filt[lane]
        for kind in (0, 1):
            own[kind, f * 8 + k if k else 96 + f, lane] = 0.5
            mirror[kind, 64 + f * 4 + (4 - k) % 4, lane] = 0.5
        own[2, f * 8 + k + 1, lane] = 0.5
        mirror[2, 64 + f * 4 + 3 - k, lane] = 0.5
        if k == 0:
            own[0, :, lane] = 0
            mirror[0, :, lane] = 0
            source = 96 + f if chan[lane] else 64 + f * 4
            own[0, source, lane] = 0.5
            mirror[0, source, lane] = 0.5
    return own.astype(BF), mirror.astype(BF)


def gather_tables():
    slot, part, kind, filt, chan = lanes()
    out = np.zeros((2, 2, 48, HALF), np.float32)
    for lane in range(HALF):
        if kind[lane]:
            continue
        for first in range(2):
            for ri in range(2):
                sign = -1.0 if ri and part[lane] else 1.0
                extra = slot[lane] == 0 and chan[lane] == 1
                if not (first and extra):
                    out[first, ri, slot[lane] * 8 + filt[lane], lane] = sign
                if extra:
                    out[first, ri, 32 + filt[lane], lane] = sign
    return out.astype(BF)


def grad_selectors():
    own = np.zeros((4, 64, 112), np.float32)
    mirror = np.zeros((4, 64, 112), np.float32)
    for f in range(8):
        for row in range(8):
            at = f * 8 + row
            for kind in (0, 1):
                if row < 4:
                    own[kind, at, row * 8 + f if row else 96 + f] = 1
                else:
                    mirror[kind, at, 48 + (7 - row) * 8 + f] = 1
            for kind in (2, 3):
                if 0 < row < 5:
                    own[kind, at, (row - 1) * 8 + f] = 1
                else:
                    mirror[kind, at, 48 + (8 - row) % 8 * 8 + f] = 1
        own[0, f * 8, 96 + f] = 0.5
        mirror[0, f * 8, 96 + f] = 0.5
        own[3, f * 8, 48 + f] = 0.5
        mirror[3, f * 8, 48 + f] = 0.5
    return own.astype(BF), mirror.astype(BF)


def payload_selectors():
    tail = np.zeros((2, 2, 16, 64), np.float32)
    head = np.zeros((8, 64), np.float32)
    for f in range(8):
        head[f, f * 8] = 1
        for row in range(4):
            tail[0, f // 4, f % 4 * 4 + row, f * 8 + 4 + row] = 1
            tail[1, f // 4, f % 4 * 4 + row, f * 8 + (4 + row if row else 0)] = 1
    return tail.astype(BF), head.astype(BF)


def dot(a, b, dims=((1,), (0,)), precision=None):
    return lax.dot_general(a, b, (dims, ((), ())), precision=precision, preferred_element_type=F32)


def turn(idx_ref, chan):
    shape = (ROWS, HALF)
    lane = lax.broadcasted_iota(jnp.int32, shape, 1)
    row = idx_ref[0] * ROWS + lax.broadcasted_iota(jnp.int32, shape, 0)
    place = lane & 63
    slot = 2 * (lane >> 7) + ((lane >> 6) & 1)
    col = 8 * place + slot + jnp.where(place >= 32, 1, jnp.where(slot == 0, 8, 0))
    if chan:
        col = jnp.where(lane == LAST, 0, col)
    phases = (row * col).astype(F32) * (-2.0 * math.pi / (N * N))
    return jnp.cos(phases), jnp.sin(phases)


def swap_first(re, im):
    first = lax.broadcasted_iota(jnp.int32, re[0].shape, 2) == LAST
    return (re[0], jnp.where(first, im[0], re[1])), (jnp.where(first, re[1], im[0]), im[1])


def kernel_a(idx_ref, rank_ref, sig_ref, cot_ref, t_ref, f_ref, tail_ref, head_ref, out_ref, tails_ref,
             heads_ref, yre, yim, z):
    upper = idx_ref[0] >> 5
    for ri in range(2):
        tails_ref[ri] = dot(tail_ref[upper, rank_ref[0] & 1], f_ref[ri]).astype(BF)
        heads_ref[ri] = dot(head_ref[...], f_ref[ri]).astype(BF)
    turns = [turn(idx_ref, chan) for chan in range(2)]
    both = dot(jnp.concatenate([sig_ref[...], cot_ref[...]], axis=0), t_ref[...])
    for half in range(2):
        part = both[half * 128 : (half + 1) * 128]
        re = part[:, :HALF].reshape(8, 2, ROWS, HALF)
        im = part[:, HALF:].reshape(8, 2, ROWS, HALF)
        re, im = swap_first((re[:, 0], re[:, 1]), (im[:, 0], im[:, 1]))
        at = pl.ds(half * 128, 128)
        out_re = [re[c] * turns[c][0] - im[c] * turns[c][1] for c in range(2)]
        out_im = [re[c] * turns[c][1] + im[c] * turns[c][0] for c in range(2)]
        for y, v in ((yre, out_re), (yim, out_im)):
            v = jnp.stack(v, axis=1).reshape(128, HALF)
            for s in range(2):
                y[s, at, :] = v[:, s * 128 : (s + 1) * 128]
    for r in range(ROWS):
        rows = [y[s, pl.ds(r, 32, stride=ROWS), :] for y in (yre, yim) for s in range(2)]
        block = jnp.concatenate(rows, axis=0).T
        for p in range(2):
            z[p, pl.ds(r, 64, stride=ROWS), :] = block[p * 64 : (p + 1) * 64]
    for p in range(2):
        out_ref[:, p * 128 : (p + 1) * 128] = z[p].astype(BF)


def kernel_f(idx_ref, rank_ref, f_ref, tail_ref, share_ref, head_ref, own_ref, mirror_ref, flip_ref, h_ref, rows):
    place = idx_ref[0]
    kind = jnp.where(place == LAST, 0, jnp.where(place < 32, 1, 2))
    rows[:, :64, :] = f_ref[...]
    half = rank_ref[0] & 1
    rows[:, pl.ds(pl.multiple_of(64 + 16 * half, 16), 16), :] = tail_ref[...]
    rows[:, pl.ds(pl.multiple_of(80 - 16 * half, 16), 16), :] = share_ref[...]
    rows[:, 96:, :] = jnp.zeros((2, 16, N), BF)
    rows[:, 96:104, :] = head_ref[...]
    lane = lax.broadcasted_iota(jnp.int32, (N, HALF), 1)
    shifted = ((lane & ~30) == 1) | ((lane & ~30) == 65)
    shifted = shifted & (place == LAST)
    negative = ((lane >> 6) & 1) == ((lane >> 4) & 1)
    for ri in range(2):
        near = dot(rows[ri], own_ref[kind], ((0,), (0,)))
        far = dot(rows[ri], mirror_ref[kind], ((0,), (0,))).astype(BF)
        far = dot(flip_ref[...], far)
        far = jnp.where(shifted, pltpu.roll(far, 1, 0), far)
        if ri == 0:
            h_ref[:, :HALF] = near + far
        else:
            value = near - far
            h_ref[:, HALF:] = jnp.where(negative, -value, value)


def kernel_b(idx_ref, r_ref, wc_ref, ws_ref, h_ref, gather_ref, v_ref, g_ref, prod):
    first = jnp.where(idx_ref[0] == LAST, 1, 0)
    sign = jnp.where(lax.broadcasted_iota(jnp.int32, (N, 128), 1) < 64, -1.0, 1.0)
    p1 = dot(wc_ref[...], r_ref[...])
    p2 = dot(ws_ref[...], r_ref[...])
    pairs = []
    for p in range(2):
        cols = slice(p * 128, (p + 1) * 128)
        x = p1[:, cols] + sign * pltpu.roll(p2[:, cols], 64, 1)
        swapped = pltpu.roll(x, 64, 1)
        h1 = h_ref[:, p * 128 : (p + 1) * 128]
        h2 = h_ref[:, HALF + p * 128 : HALF + (p + 1) * 128]
        prod[:, cols] = (h1 * x + h2 * swapped).astype(BF)
        pairs.append((pltpu.roll(x, 112, 1) * x, pltpu.roll(x, 48, 1) * x))
    for ri in range(2):
        terms = jnp.concatenate([pairs[0][ri], pairs[1][ri]], axis=1)
        high = terms.astype(BF)
        low = (terms - high.astype(F32)).astype(BF)
        take = gather_ref[first, ri]
        total = dot(take, high, ((1,), (1,))) + dot(take, low, ((1,), (1,)))
        g_ref[ri] = total.astype(BF)
    q1 = dot(wc_ref[...], prod[...])
    q2 = dot(ws_ref[...], prod[...])
    for p in range(2):
        cols = slice(p * 128, (p + 1) * 128)
        v_ref[:, cols] = (q1[:, cols] - sign * pltpu.roll(q2[:, cols], 64, 1)).astype(BF)


def kernel_c(idx_ref, v_ref, t_ref, out_ref, grad_ref, z, yre, yim):
    for p in range(2):
        z[p] = v_ref[:, p * 128 : (p + 1) * 128].astype(F32)
    for r in range(ROWS):
        rows = [z[p, pl.ds(r, 64, stride=ROWS), :] for p in range(2)]
        block = jnp.concatenate(rows, axis=0).T
        for ri, y in enumerate((yre, yim)):
            for s in range(2):
                at = ri * 64 + s * 32
                y[s, pl.ds(r, 32, stride=ROWS), :] = block[at : at + 32]
    double = jnp.where(lax.broadcasted_iota(jnp.int32, (ROWS, HALF), 1) == LAST, 1.0, 2.0)
    turns = [[t * double for t in turn(idx_ref, chan)] for chan in range(2)]
    for half, ref in enumerate((out_ref, grad_ref)):
        at = pl.ds(half * 128, 128)
        re, im = (
            jnp.concatenate([y[s, at, :] for s in range(2)], axis=1).reshape(8, 2, ROWS, HALF)
            for y in (yre, yim)
        )
        mid_re = [re[:, c] * turns[c][0] + im[:, c] * turns[c][1] for c in range(2)]
        mid_im = [im[:, c] * turns[c][0] - re[:, c] * turns[c][1] for c in range(2)]
        mid_re, mid_im = (
            jnp.stack(v, axis=1).reshape(128, HALF).astype(BF) for v in swap_first(mid_re, mid_im)
        )
        total = dot(mid_re, t_ref[:, :HALF], ((1,), (1,)))
        total = total + dot(mid_im, t_ref[:, HALF:], ((1,), (1,)))
        ref[...] = total.astype(BF)


def kernel_g(idx_ref, g_ref, far_ref, head_ref, own_ref, mirror_ref, flip_ref, out_ref, rows):
    place = idx_ref[0]
    kind = jnp.where(
        place == 0, 0, jnp.where(place == 32, 3, jnp.where(place < 32, 1, 2))
    )
    rows[:, :48, :] = g_ref[...]
    rows[:, 48:80, :] = far_ref[...]
    rows[:, 80:96, :] = jnp.zeros((2, 16, N), BF)
    rows[:, 96:, :] = jnp.zeros((2, 16, N), BF)
    rows[:, 96:104, :] = head_ref[...]
    row = lax.broadcasted_iota(jnp.int32, (64, N), 0)
    shifted = ((row & 7) == 0) & (place == 0)
    for ri in range(2):
        near = dot(own_ref[kind], rows[ri])
        far = dot(mirror_ref[kind], rows[ri]).astype(BF)
        far = dot(far, flip_ref[...])
        far = jnp.where(shifted, pltpu.roll(far, 1, 1), far)
        out_ref[ri] = (near + far if ri == 0 else near - far).astype(BF)


def body(signal, cotangent, filter_spec):
    shape = signal.shape
    place = lax.axis_index("seq").astype(jnp.int32).reshape(1)
    rank = lax.axis_index("dp").astype(jnp.int32).reshape(1)
    table = jnp.asarray(first_table())
    cos_t, sin_t = (jnp.asarray(t) for t in unit_tables())
    flip = jnp.asarray(np.eye(N, dtype=np.float32)[::-1].astype(BF))
    tail, head = (jnp.asarray(t) for t in payload_selectors())
    f_own, f_mirror = (jnp.asarray(t) for t in filter_selectors())
    g_own, g_mirror = (jnp.asarray(t) for t in grad_selectors())
    gather = jnp.asarray(gather_tables())
    opposite = [(d, SEQ - 1 - d) for d in range(SEQ)]
    down = [(d, d // 32 * 32 + (d - 1) % 32) for d in range(SEQ)]
    up = [(b, a) for a, b in down]
    filt = filter_spec.reshape(2, 64, N)
    sent, tails, heads = pl.pallas_call(
        kernel_a,
        in_specs=[SMEM] * 2 + [VMEM] * 6,
        out_specs=[VMEM] * 3,
        out_shape=[
            jax.ShapeDtypeStruct((N, HALF), BF),
            jax.ShapeDtypeStruct((2, 16, N), BF),
            jax.ShapeDtypeStruct((2, 8, N), BF),
        ],
        scratch_shapes=[
            pltpu.VMEM((2, 256, 128), F32),
            pltpu.VMEM((2, 256, 128), F32),
            pltpu.VMEM((2, N, 128), F32),
        ],
    )(place, rank, signal.reshape(128, N), cotangent.reshape(128, N), table, filt, tail, head)
    got = lax.all_to_all(sent.reshape(SEQ, ROWS, HALF), "seq", 0, 0, tiled=True)
    tails = lax.ppermute(tails, "seq", opposite)
    heads = lax.ppermute(heads, "seq", down)
    share = lax.ppermute(tails, "dp", [(d, d ^ 1) for d in range(8)])
    spread = pl.pallas_call(
        kernel_f,
        in_specs=[SMEM] * 2 + [VMEM] * 7,
        out_specs=VMEM,
        out_shape=jax.ShapeDtypeStruct((N, N), F32),
        scratch_shapes=[pltpu.VMEM((2, 112, N), BF)],
        compiler_params=PARAMS,
        cost_estimate=pl.CostEstimate(flops=400000000, bytes_accessed=2000000, transcendentals=0),
    )(place, rank, filt, tails, share, heads, f_own, f_mirror, flip)
    back, grad = pl.pallas_call(
        kernel_b,
        in_specs=[SMEM] + [VMEM] * 5,
        out_specs=[VMEM, VMEM],
        out_shape=[
            jax.ShapeDtypeStruct((N, HALF), BF),
            jax.ShapeDtypeStruct((2, 48, N), BF),
        ],
        scratch_shapes=[pltpu.VMEM((N, HALF), BF)],
        compiler_params=PARAMS,
    )(place, got.reshape(N, HALF), cos_t, sin_t, spread, gather)
    far = lax.ppermute(grad[:, :32], "seq", opposite)
    slot = jnp.where(place[0] == LAST, grad[:, 32:40], grad[:, :8])
    slot = lax.ppermute(slot, "seq", up)
    mid = lax.all_to_all(back.reshape(SEQ, ROWS, HALF), "seq", 0, 0, tiled=True)
    grad = pl.pallas_call(
        kernel_g,
        in_specs=[SMEM] + [VMEM] * 6,
        out_specs=VMEM,
        out_shape=jax.ShapeDtypeStruct((2, 64, N), BF),
        scratch_shapes=[pltpu.VMEM((2, 112, N), BF)],
        compiler_params=PARAMS,
        cost_estimate=pl.CostEstimate(flops=100000000, bytes_accessed=1000000, transcendentals=0),
    )(place, grad, far, slot, g_own, g_mirror, flip)
    for bit in (2, 4, 1):
        other = lax.ppermute(grad, "dp", [(d, d ^ bit) for d in range(8)])
        grad = (grad.astype(F32) + other.astype(F32)).astype(BF)
    output, grad_signal = pl.pallas_call(
        kernel_c,
        in_specs=[SMEM, VMEM, VMEM],
        out_specs=[VMEM, VMEM],
        out_shape=[jax.ShapeDtypeStruct((128, N), BF)] * 2,
        scratch_shapes=[
            pltpu.VMEM((2, N, 128), F32),
            pltpu.VMEM((2, 256, 128), F32),
            pltpu.VMEM((2, 256, 128), F32),
        ],
        compiler_params=PARAMS,
        cost_estimate=pl.CostEstimate(flops=400000000, bytes_accessed=2000000, transcendentals=0),
    )(place, mid.reshape(N, HALF), table)
    return output.reshape(shape), grad_signal.reshape(shape), grad.reshape(2, 8, 8, N)


def solution(mesh):
    placed = (P(None, "dp", "seq", None), P(None, "dp", "seq", None), P(None, None, "seq", None))
    return jax.shard_map(body, mesh=mesh, in_specs=placed, out_specs=placed, check_vma=False)
```

```python
import math

import jax
import jax.numpy as jnp
import numpy as np
from jax import lax
from jax.experimental import pallas as pl
from jax.experimental.pallas import tpu as pltpu
from jax.sharding import PartitionSpec as P

N = 512
SEQ = 64
ROWS = N // SEQ
HALF = N // 2
BF = jnp.bfloat16
F32 = jnp.float32
VMEM = pl.BlockSpec(memory_space=pltpu.VMEM)
SMEM = pl.BlockSpec(memory_space=pltpu.SMEM)
HBM = pl.BlockSpec(memory_space=pltpu.HBM)
PARAMS = pltpu.CompilerParams(vmem_limit_bytes=20 * 2**20)

LAST = 31


def unit_tables():
    steps = np.arange(N, dtype=np.int32)
    phases = (steps[:, None] * steps[None, :] % N).astype(np.float32) * np.float32(
        2.0 * math.pi / N
    )
    factor = np.float32(1.0 / math.sqrt(N))
    return (np.cos(phases) * factor).astype(BF), (-np.sin(phases) * factor).astype(BF)


def first_table():
    cos_t, sin_t = unit_tables()
    col = np.arange(HALF)
    place = col % 64
    slot = 2 * (col // 128) + col // 64 % 2
    row = 8 * place + slot + np.where(place >= 32, 1, 8 * (slot == 0))
    re, im = cos_t[:, row], sin_t[:, row]
    im[:, LAST] = cos_t[:, 0]
    return np.concatenate([re, im], axis=1)


def lanes():
    lane = np.arange(HALF)
    slot = 2 * (lane // 32 % 2) + lane // 128
    return slot, lane // 64 % 2, lane // 16 % 2, lane // 2 % 8, lane % 2


def filter_selectors():
    slot, _, _, filt, chan = lanes()
    own = np.zeros((3, 112, HALF), np.float32)
    mirror = np.zeros((3, 112, HALF), np.float32)
    for lane in range(HALF):
        k, f = slot[lane], filt[lane]
        for kind in (0, 1):
            own[kind, f * 8 + k if k else 96 + f, lane] = 0.5
            mirror[kind, 64 + f * 4 + (4 - k) % 4, lane] = 0.5
        own[2, f * 8 + k + 1, lane] = 0.5
        mirror[2, 64 + f * 4 + 3 - k, lane] = 0.5
        if k == 0:
            own[0, :, lane] = 0
            mirror[0, :, lane] = 0
            source = 96 + f if chan[lane] else 64 + f * 4
            own[0, source, lane] = 0.5
            mirror[0, source, lane] = 0.5
    return own.astype(BF), mirror.astype(BF)


def gather_tables():
    slot, part, kind, filt, chan = lanes()
    out = np.zeros((2, 2, 48, HALF), np.float32)
    for lane in range(HALF):
        if kind[lane]:
            continue
        for first in range(2):
            for ri in range(2):
                sign = -1.0 if ri and part[lane] else 1.0
                extra = slot[lane] == 0 and chan[lane] == 1
                if not (first and extra):
                    out[first, ri, slot[lane] * 8 + filt[lane], lane] = sign
                if extra:
                    out[first, ri, 32 + filt[lane], lane] = sign
    return out.astype(BF)


def grad_selectors():
    own = np.zeros((4, 64, 112), np.float32)
    mirror = np.zeros((4, 64, 112), np.float32)
    for f in range(8):
        for row in range(8):
            at = f * 8 + row
            for kind in (0, 1):
                if row < 4:
                    own[kind, at, row * 8 + f if row else 96 + f] = 1
                else:
                    mirror[kind, at, 48 + (7 - row) * 8 + f] = 1
            for kind in (2, 3):
                if 0 < row < 5:
                    own[kind, at, (row - 1) * 8 + f] = 1
                else:
                    mirror[kind, at, 48 + (8 - row) % 8 * 8 + f] = 1
        own[0, f * 8, 96 + f] = 0.5
        mirror[0, f * 8, 96 + f] = 0.5
        own[3, f * 8, 48 + f] = 0.5
        mirror[3, f * 8, 48 + f] = 0.5
    return own.astype(BF), mirror.astype(BF)


def payload_selectors():
    tail = np.zeros((2, 32, 64), np.float32)
    head = np.zeros((8, 64), np.float32)
    for f in range(8):
        head[f, f * 8] = 1
        for row in range(4):
            tail[0, f * 4 + row, f * 8 + 4 + row] = 1
            tail[1, f * 4 + row, f * 8 + (4 + row if row else 0)] = 1
    return tail.astype(BF), head.astype(BF)


def dot(a, b, dims=((1,), (0,)), precision=None):
    return lax.dot_general(a, b, (dims, ((), ())), precision=precision, preferred_element_type=F32)


def turn(idx_ref, chan):
    shape = (ROWS, HALF)
    lane = lax.broadcasted_iota(jnp.int32, shape, 1)
    row = idx_ref[0] * ROWS + lax.broadcasted_iota(jnp.int32, shape, 0)
    place = lane & 63
    slot = 2 * (lane >> 7) + ((lane >> 6) & 1)
    col = 8 * place + slot + jnp.where(place >= 32, 1, jnp.where(slot == 0, 8, 0))
    if chan:
        col = jnp.where(lane == LAST, 0, col)
    phases = (row * col).astype(F32) * (-2.0 * math.pi / (N * N))
    return jnp.cos(phases), jnp.sin(phases)


def swap_first(re, im):
    first = lax.broadcasted_iota(jnp.int32, re[0].shape, 2) == LAST
    return (re[0], jnp.where(first, im[0], re[1])), (jnp.where(first, re[1], im[0]), im[1])


def kernel_a(idx_ref, sig_hbm, cot_hbm, t_hbm, f_hbm, tail_hbm, head_hbm, out_ref, tails_ref,
             heads_ref, x_ref, t_ref, f_ref, tail_ref, head_ref, yre, yim, z, sems):
    moves = (
        (sig_hbm, x_ref.at[pl.ds(0, 128)]),
        (cot_hbm, x_ref.at[pl.ds(128, 128)]),
        (t_hbm, t_ref),
        (f_hbm, f_ref),
        (tail_hbm, tail_ref),
        (head_hbm, head_ref),
    )
    copies = [pltpu.make_async_copy(a, b, sems.at[k]) for k, (a, b) in enumerate(moves)]
    for copy in copies:
        copy.start()
    turns = [turn(idx_ref, chan) for chan in range(2)]
    for copy in copies:
        copy.wait()
    upper = idx_ref[0] >> 5
    for ri in range(2):
        tails_ref[ri] = dot(tail_ref[upper], f_ref[ri]).astype(BF)
        heads_ref[ri] = dot(head_ref[...], f_ref[ri]).astype(BF)
    both = dot(x_ref[...], t_ref[...])
    for half in range(2):
        part = both[half * 128 : (half + 1) * 128]
        re = part[:, :HALF].reshape(8, 2, ROWS, HALF)
        im = part[:, HALF:].reshape(8, 2, ROWS, HALF)
        re, im = swap_first((re[:, 0], re[:, 1]), (im[:, 0], im[:, 1]))
        at = pl.ds(half * 128, 128)
        out_re = [re[c] * turns[c][0] - im[c] * turns[c][1] for c in range(2)]
        out_im = [re[c] * turns[c][1] + im[c] * turns[c][0] for c in range(2)]
        for y, v in ((yre, out_re), (yim, out_im)):
            v = jnp.stack(v, axis=1).reshape(128, HALF)
            for s in range(2):
                y[s, at, :] = v[:, s * 128 : (s + 1) * 128]
    for r in range(ROWS):
        rows = [y[s, pl.ds(r, 32, stride=ROWS), :] for y in (yre, yim) for s in range(2)]
        block = jnp.concatenate(rows, axis=0).T
        for p in range(2):
            z[p, pl.ds(r, 64, stride=ROWS), :] = block[p * 64 : (p + 1) * 64]
    for p in range(2):
        out_ref[:, p * 128 : (p + 1) * 128] = z[p].astype(BF)


def kernel_f(idx_ref, f_ref, tail_ref, head_ref, own_ref, mirror_ref, flip_ref, h_ref, rows):
    place = idx_ref[0]
    kind = jnp.where(place == LAST, 0, jnp.where(place < 32, 1, 2))
    rows[:, :64, :] = f_ref[...]
    rows[:, 64:96, :] = tail_ref[...]
    rows[:, 96:, :] = jnp.zeros((2, 16, N), BF)
    rows[:, 96:104, :] = head_ref[...]
    lane = lax.broadcasted_iota(jnp.int32, (N, HALF), 1)
    shifted = ((lane & ~30) == 1) | ((lane & ~30) == 65)
    shifted = shifted & (place == LAST)
    negative = ((lane >> 6) & 1) == ((lane >> 4) & 1)
    for ri in range(2):
        near = dot(rows[ri], own_ref[kind], ((0,), (0,)))
        far = dot(rows[ri], mirror_ref[kind], ((0,), (0,))).astype(BF)
        far = dot(flip_ref[...], far)
        far = jnp.where(shifted, pltpu.roll(far, 1, 0), far)
        if ri == 0:
            h_ref[:, :HALF] = near + far
        else:
            value = near - far
            h_ref[:, HALF:] = jnp.where(negative, -value, value)


def kernel_b(idx_ref, r_ref, wc_ref, ws_ref, h_ref, gather_ref, v_ref, g_ref, prod):
    first = jnp.where(idx_ref[0] == LAST, 1, 0)
    sign = jnp.where(lax.broadcasted_iota(jnp.int32, (N, 128), 1) < 64, -1.0, 1.0)
    p1 = dot(wc_ref[...], r_ref[...])
    p2 = dot(ws_ref[...], r_ref[...])
    pairs = []
    for p in range(2):
        cols = slice(p * 128, (p + 1) * 128)
        x = p1[:, cols] + sign * pltpu.roll(p2[:, cols], 64, 1)
        swapped = pltpu.roll(x, 64, 1)
        h1 = h_ref[:, p * 128 : (p + 1) * 128]
        h2 = h_ref[:, HALF + p * 128 : HALF + (p + 1) * 128]
        prod[:, cols] = (h1 * x + h2 * swapped).astype(BF)
        pairs.append((pltpu.roll(x, 112, 1) * x, pltpu.roll(x, 48, 1) * x))
    for ri in range(2):
        terms = jnp.concatenate([pairs[0][ri], pairs[1][ri]], axis=1)
        high = terms.astype(BF)
        low = (terms - high.astype(F32)).astype(BF)
        take = gather_ref[first, ri]
        total = dot(take, high, ((1,), (1,))) + dot(take, low, ((1,), (1,)))
        g_ref[ri] = total.astype(BF)
    q1 = dot(wc_ref[...], prod[...])
    q2 = dot(ws_ref[...], prod[...])
    for p in range(2):
        cols = slice(p * 128, (p + 1) * 128)
        v_ref[:, cols] = (q1[:, cols] - sign * pltpu.roll(q2[:, cols], 64, 1)).astype(BF)


def kernel_c(idx_ref, v_ref, t_ref, out_ref, grad_ref, z, yre, yim):
    for p in range(2):
        z[p] = v_ref[:, p * 128 : (p + 1) * 128].astype(F32)
    for r in range(ROWS):
        rows = [z[p, pl.ds(r, 64, stride=ROWS), :] for p in range(2)]
        block = jnp.concatenate(rows, axis=0).T
        for ri, y in enumerate((yre, yim)):
            for s in range(2):
                at = ri * 64 + s * 32
                y[s, pl.ds(r, 32, stride=ROWS), :] = block[at : at + 32]
    double = jnp.where(lax.broadcasted_iota(jnp.int32, (ROWS, HALF), 1) == LAST, 1.0, 2.0)
    turns = [[t * double for t in turn(idx_ref, chan)] for chan in range(2)]
    for half, ref in enumerate((out_ref, grad_ref)):
        at = pl.ds(half * 128, 128)
        re, im = (
            jnp.concatenate([y[s, at, :] for s in range(2)], axis=1).reshape(8, 2, ROWS, HALF)
            for y in (yre, yim)
        )
        mid_re = [re[:, c] * turns[c][0] + im[:, c] * turns[c][1] for c in range(2)]
        mid_im = [im[:, c] * turns[c][0] - re[:, c] * turns[c][1] for c in range(2)]
        mid_re, mid_im = (
            jnp.stack(v, axis=1).reshape(128, HALF).astype(BF) for v in swap_first(mid_re, mid_im)
        )
        total = dot(mid_re, t_ref[:, :HALF], ((1,), (1,)))
        total = total + dot(mid_im, t_ref[:, HALF:], ((1,), (1,)))
        ref[...] = total.astype(BF)


def kernel_g(idx_ref, g_ref, far_ref, head_ref, own_ref, mirror_ref, flip_ref, out_ref, rows):
    place = idx_ref[0]
    kind = jnp.where(
        place == 0, 0, jnp.where(place == 32, 3, jnp.where(place < 32, 1, 2))
    )
    rows[:, :48, :] = g_ref[...]
    rows[:, 48:80, :] = far_ref[...]
    rows[:, 80:96, :] = jnp.zeros((2, 16, N), BF)
    rows[:, 96:, :] = jnp.zeros((2, 16, N), BF)
    rows[:, 96:104, :] = head_ref[...]
    row = lax.broadcasted_iota(jnp.int32, (64, N), 0)
    shifted = ((row & 7) == 0) & (place == 0)
    for ri in range(2):
        near = dot(own_ref[kind], rows[ri])
        far = dot(mirror_ref[kind], rows[ri]).astype(BF)
        far = dot(far, flip_ref[...])
        far = jnp.where(shifted, pltpu.roll(far, 1, 1), far)
        out_ref[ri] = (near + far if ri == 0 else near - far).astype(BF)


def body(signal, cotangent, filter_spec):
    shape = signal.shape
    place = lax.axis_index("seq").astype(jnp.int32).reshape(1)
    table = jnp.asarray(first_table())
    cos_t, sin_t = (jnp.asarray(t) for t in unit_tables())
    flip = jnp.asarray(np.eye(N, dtype=np.float32)[::-1].astype(BF))
    tail, head = (jnp.asarray(t) for t in payload_selectors())
    f_own, f_mirror = (jnp.asarray(t) for t in filter_selectors())
    g_own, g_mirror = (jnp.asarray(t) for t in grad_selectors())
    gather = jnp.asarray(gather_tables())
    opposite = [(d, SEQ - 1 - d) for d in range(SEQ)]
    down = [(d, d // 32 * 32 + (d - 1) % 32) for d in range(SEQ)]
    up = [(b, a) for a, b in down]
    filt = filter_spec.reshape(2, 64, N)
    sent, tails, heads = pl.pallas_call(
        kernel_a,
        in_specs=[SMEM] + [HBM] * 6,
        out_specs=[VMEM] * 3,
        out_shape=[
            jax.ShapeDtypeStruct((N, HALF), BF),
            jax.ShapeDtypeStruct((2, 32, N), BF),
            jax.ShapeDtypeStruct((2, 8, N), BF),
        ],
        scratch_shapes=[
            pltpu.VMEM((256, N), BF),
            pltpu.VMEM((N, N), BF),
            pltpu.VMEM((2, 64, N), BF),
            pltpu.VMEM((2, 32, 64), BF),
            pltpu.VMEM((8, 64), BF),
            pltpu.VMEM((2, 256, 128), F32),
            pltpu.VMEM((2, 256, 128), F32),
            pltpu.VMEM((2, N, 128), F32),
            pltpu.SemaphoreType.DMA((6,)),
        ],
    )(place, signal.reshape(128, N), cotangent.reshape(128, N), table, filt, tail, head)
    got = lax.all_to_all(sent.reshape(SEQ, ROWS, HALF), "seq", 0, 0, tiled=True)
    tails = lax.ppermute(tails, "seq", opposite)
    heads = lax.ppermute(heads, "seq", down)
    spread = pl.pallas_call(
        kernel_f,
        in_specs=[SMEM] + [VMEM] * 6,
        out_specs=VMEM,
        out_shape=jax.ShapeDtypeStruct((N, N), F32),
        scratch_shapes=[pltpu.VMEM((2, 112, N), BF)],
        compiler_params=PARAMS,
        cost_estimate=pl.CostEstimate(flops=400000000, bytes_accessed=2000000, transcendentals=0),
    )(place, filt, tails, heads, f_own, f_mirror, flip)
    back, grad = pl.pallas_call(
        kernel_b,
        in_specs=[SMEM] + [VMEM] * 5,
        out_specs=[VMEM, VMEM],
        out_shape=[
            jax.ShapeDtypeStruct((N, HALF), BF),
            jax.ShapeDtypeStruct((2, 48, N), BF),
        ],
        scratch_shapes=[pltpu.VMEM((N, HALF), BF)],
        compiler_params=PARAMS,
    )(place, got.reshape(N, HALF), cos_t, sin_t, spread, gather)
    far = lax.ppermute(grad[:, :32], "seq", opposite)
    slot = jnp.where(place[0] == LAST, grad[:, 32:40], grad[:, :8])
    slot = lax.ppermute(slot, "seq", up)
    mid = lax.all_to_all(back.reshape(SEQ, ROWS, HALF), "seq", 0, 0, tiled=True)
    grad = pl.pallas_call(
        kernel_g,
        in_specs=[SMEM] + [VMEM] * 6,
        out_specs=VMEM,
        out_shape=jax.ShapeDtypeStruct((2, 64, N), BF),
        scratch_shapes=[pltpu.VMEM((2, 112, N), BF)],
        compiler_params=PARAMS,
        cost_estimate=pl.CostEstimate(flops=100000000, bytes_accessed=1000000, transcendentals=0),
    )(place, grad, far, slot, g_own, g_mirror, flip)
    for bit in (2, 4, 1):
        other = lax.ppermute(grad, "dp", [(d, d ^ bit) for d in range(8)])
        grad = (grad.astype(F32) + other.astype(F32)).astype(BF)
    output, grad_signal = pl.pallas_call(
        kernel_c,
        in_specs=[SMEM, VMEM, VMEM],
        out_specs=[VMEM, VMEM],
        out_shape=[jax.ShapeDtypeStruct((128, N), BF)] * 2,
        scratch_shapes=[
            pltpu.VMEM((2, N, 128), F32),
            pltpu.VMEM((2, 256, 128), F32),
            pltpu.VMEM((2, 256, 128), F32),
        ],
        compiler_params=PARAMS,
        cost_estimate=pl.CostEstimate(flops=400000000, bytes_accessed=2000000, transcendentals=0),
    )(place, mid.reshape(N, HALF), table)
    return output.reshape(shape), grad_signal.reshape(shape), grad.reshape(2, 8, 8, N)


def solution(mesh):
    placed = (P(None, "dp", "seq", None), P(None, "dp", "seq", None), P(None, None, "seq", None))
    return jax.shard_map(body, mesh=mesh, in_specs=placed, out_specs=placed, check_vma=False)
```

```python
import math

import jax
import jax.numpy as jnp
import numpy as np
from jax import lax
from jax.experimental import pallas as pl
from jax.experimental.pallas import tpu as pltpu
from jax.sharding import PartitionSpec as P

N = 512
SEQ = 64
ROWS = N // SEQ
HALF = N // 2
BF = jnp.bfloat16
F32 = jnp.float32
VMEM = pl.BlockSpec(memory_space=pltpu.VMEM)
SMEM = pl.BlockSpec(memory_space=pltpu.SMEM)
PARAMS = pltpu.CompilerParams(vmem_limit_bytes=20 * 2**20)

LAST = 31


def unit_tables():
    steps = np.arange(N, dtype=np.int32)
    phases = (steps[:, None] * steps[None, :] % N).astype(np.float32) * np.float32(
        2.0 * math.pi / N
    )
    factor = np.float32(1.0 / math.sqrt(N))
    return (np.cos(phases) * factor).astype(BF), (-np.sin(phases) * factor).astype(BF)


def first_table():
    cos_t, sin_t = unit_tables()
    col = np.arange(HALF)
    place = col % 64
    slot = 2 * (col // 128) + col // 64 % 2
    row = 8 * place + slot + np.where(place >= 32, 1, 8 * (slot == 0))
    re, im = cos_t[:, row], sin_t[:, row]
    im[:, LAST] = cos_t[:, 0]
    return np.concatenate([re, im], axis=1)


def lanes():
    lane = np.arange(HALF)
    slot = 2 * (lane // 32 % 2) + lane // 128
    return slot, lane // 64 % 2, lane // 16 % 2, lane // 2 % 8, lane % 2


def filter_selectors():
    slot, _, _, filt, chan = lanes()
    own = np.zeros((3, 112, HALF), np.float32)
    mirror = np.zeros((3, 112, HALF), np.float32)
    for lane in range(HALF):
        k, f = slot[lane], filt[lane]
        for kind in (0, 1):
            own[kind, f * 8 + k if k else 96 + f, lane] = 0.5
            mirror[kind, 64 + f * 4 + (4 - k) % 4, lane] = 0.5
        own[2, f * 8 + k + 1, lane] = 0.5
        mirror[2, 64 + f * 4 + 3 - k, lane] = 0.5
        if k == 0:
            own[0, :, lane] = 0
            mirror[0, :, lane] = 0
            source = 96 + f if chan[lane] else 64 + f * 4
            own[0, source, lane] = 0.5
            mirror[0, source, lane] = 0.5
    return own.astype(BF), mirror.astype(BF)


def gather_tables():
    slot, part, kind, filt, chan = lanes()
    out = np.zeros((2, 2, 48, HALF), np.float32)
    for lane in range(HALF):
        if kind[lane]:
            continue
        for first in range(2):
            for ri in range(2):
                sign = -1.0 if ri and part[lane] else 1.0
                extra = slot[lane] == 0 and chan[lane] == 1
                if not (first and extra):
                    out[first, ri, slot[lane] * 8 + filt[lane], lane] = sign
                if extra:
                    out[first, ri, 32 + filt[lane], lane] = sign
    return out.astype(BF)


def grad_selectors():
    own = np.zeros((4, 64, 112), np.float32)
    mirror = np.zeros((4, 64, 112), np.float32)
    for f in range(8):
        for row in range(8):
            at = f * 8 + row
            for kind in (0, 1):
                if row < 4:
                    own[kind, at, row * 8 + f if row else 96 + f] = 1
                else:
                    mirror[kind, at, 48 + (7 - row) * 8 + f] = 1
            for kind in (2, 3):
                if 0 < row < 5:
                    own[kind, at, (row - 1) * 8 + f] = 1
                else:
                    mirror[kind, at, 48 + (8 - row) % 8 * 8 + f] = 1
        own[0, f * 8, 96 + f] = 0.5
        mirror[0, f * 8, 96 + f] = 0.5
        own[3, f * 8, 48 + f] = 0.5
        mirror[3, f * 8, 48 + f] = 0.5
    return own.astype(BF), mirror.astype(BF)


def payload_selectors():
    tail = np.zeros((2, 32, 64), np.float32)
    head = np.zeros((8, 64), np.float32)
    for f in range(8):
        head[f, f * 8] = 1
        for row in range(4):
            tail[0, f * 4 + row, f * 8 + 4 + row] = 1
            tail[1, f * 4 + row, f * 8 + (4 + row if row else 0)] = 1
    return tail.astype(BF), head.astype(BF)


def dot(a, b, dims=((1,), (0,)), precision=None):
    return lax.dot_general(a, b, (dims, ((), ())), precision=precision, preferred_element_type=F32)


def turn(idx_ref, chan):
    shape = (ROWS, HALF)
    lane = lax.broadcasted_iota(jnp.int32, shape, 1)
    row = idx_ref[0] * ROWS + lax.broadcasted_iota(jnp.int32, shape, 0)
    place = lane & 63
    slot = 2 * (lane >> 7) + ((lane >> 6) & 1)
    col = 8 * place + slot + jnp.where(place >= 32, 1, jnp.where(slot == 0, 8, 0))
    if chan:
        col = jnp.where(lane == LAST, 0, col)
    phases = (row * col).astype(F32) * (-2.0 * math.pi / (N * N))
    return jnp.cos(phases), jnp.sin(phases)


def swap_first(re, im):
    first = lax.broadcasted_iota(jnp.int32, re[0].shape, 2) == LAST
    return (re[0], jnp.where(first, im[0], re[1])), (jnp.where(first, re[1], im[0]), im[1])


def kernel_a(idx_ref, sig_ref, cot_ref, t_ref, f_ref, tail_ref, head_ref, out_ref, tails_ref,
             heads_ref, yre, yim, z):
    upper = idx_ref[0] >> 5
    for ri in range(2):
        tails_ref[ri] = dot(tail_ref[upper], f_ref[ri]).astype(BF)
        heads_ref[ri] = dot(head_ref[...], f_ref[ri]).astype(BF)
    turns = [turn(idx_ref, chan) for chan in range(2)]
    both = dot(jnp.concatenate([sig_ref[...], cot_ref[...]], axis=0), t_ref[...])
    for half in range(2):
        part = both[half * 128 : (half + 1) * 128]
        re = part[:, :HALF].reshape(8, 2, ROWS, HALF)
        im = part[:, HALF:].reshape(8, 2, ROWS, HALF)
        re, im = swap_first((re[:, 0], re[:, 1]), (im[:, 0], im[:, 1]))
        at = pl.ds(half * 128, 128)
        out_re = [re[c] * turns[c][0] - im[c] * turns[c][1] for c in range(2)]
        out_im = [re[c] * turns[c][1] + im[c] * turns[c][0] for c in range(2)]
        for y, v in ((yre, out_re), (yim, out_im)):
            v = jnp.stack(v, axis=1).reshape(128, HALF)
            for s in range(2):
                y[s, at, :] = v[:, s * 128 : (s + 1) * 128]
    for r in range(ROWS):
        rows = [y[s, pl.ds(r, 32, stride=ROWS), :] for y in (yre, yim) for s in range(2)]
        block = jnp.concatenate(rows, axis=0).T
        for p in range(2):
            z[p, pl.ds(r, 64, stride=ROWS), :] = block[p * 64 : (p + 1) * 64]
    for p in range(2):
        out_ref[:, p * 128 : (p + 1) * 128] = z[p].astype(BF)


def kernel_f(idx_ref, f_ref, tail_ref, head_ref, own_ref, mirror_ref, flip_ref, h_ref, rows):
    place = idx_ref[0]
    kind = jnp.where(place == LAST, 0, jnp.where(place < 32, 1, 2))
    rows[:, :64, :] = f_ref[...]
    rows[:, 64:96, :] = tail_ref[...]
    rows[:, 96:, :] = jnp.zeros((2, 16, N), BF)
    rows[:, 96:104, :] = head_ref[...]
    lane = lax.broadcasted_iota(jnp.int32, (N, HALF), 1)
    shifted = ((lane & ~30) == 1) | ((lane & ~30) == 65)
    shifted = shifted & (place == LAST)
    negative = ((lane >> 6) & 1) == ((lane >> 4) & 1)
    for ri in range(2):
        near = dot(rows[ri], own_ref[kind], ((0,), (0,)))
        far = dot(rows[ri], mirror_ref[kind], ((0,), (0,))).astype(BF)
        far = dot(flip_ref[...], far)
        far = jnp.where(shifted, pltpu.roll(far, 1, 0), far)
        if ri == 0:
            h_ref[:, :HALF] = near + far
        else:
            value = near - far
            h_ref[:, HALF:] = jnp.where(negative, -value, value)


def kernel_b(idx_ref, r_ref, wc_ref, ws_ref, h_ref, gather_ref, v_ref, g_ref, prod):
    first = jnp.where(idx_ref[0] == LAST, 1, 0)
    sign = jnp.where(lax.broadcasted_iota(jnp.int32, (N, 128), 1) < 64, -1.0, 1.0)
    p1 = dot(wc_ref[...], r_ref[...])
    p2 = dot(ws_ref[...], r_ref[...])
    pairs = []
    for p in range(2):
        cols = slice(p * 128, (p + 1) * 128)
        x = p1[:, cols] + sign * pltpu.roll(p2[:, cols], 64, 1)
        swapped = pltpu.roll(x, 64, 1)
        h1 = h_ref[:, p * 128 : (p + 1) * 128]
        h2 = h_ref[:, HALF + p * 128 : HALF + (p + 1) * 128]
        prod[:, cols] = (h1 * x + h2 * swapped).astype(BF)
        pairs.append((pltpu.roll(x, 112, 1) * x, pltpu.roll(x, 48, 1) * x))
    for ri in range(2):
        terms = jnp.concatenate([pairs[0][ri], pairs[1][ri]], axis=1)
        g_ref[ri] = dot(gather_ref[first, ri], terms.astype(BF), ((1,), (1,))).astype(BF)
    q1 = dot(wc_ref[...], prod[...])
    q2 = dot(ws_ref[...], prod[...])
    for p in range(2):
        cols = slice(p * 128, (p + 1) * 128)
        v_ref[:, cols] = (q1[:, cols] - sign * pltpu.roll(q2[:, cols], 64, 1)).astype(BF)


def kernel_c(idx_ref, v_ref, t_ref, out_ref, grad_ref, z, yre, yim):
    for p in range(2):
        z[p] = v_ref[:, p * 128 : (p + 1) * 128].astype(F32)
    for r in range(ROWS):
        rows = [z[p, pl.ds(r, 64, stride=ROWS), :] for p in range(2)]
        block = jnp.concatenate(rows, axis=0).T
        for ri, y in enumerate((yre, yim)):
            for s in range(2):
                at = ri * 64 + s * 32
                y[s, pl.ds(r, 32, stride=ROWS), :] = block[at : at + 32]
    double = jnp.where(lax.broadcasted_iota(jnp.int32, (ROWS, HALF), 1) == LAST, 1.0, 2.0)
    turns = [[t * double for t in turn(idx_ref, chan)] for chan in range(2)]
    for half, ref in enumerate((out_ref, grad_ref)):
        at = pl.ds(half * 128, 128)
        re, im = (
            jnp.concatenate([y[s, at, :] for s in range(2)], axis=1).reshape(8, 2, ROWS, HALF)
            for y in (yre, yim)
        )
        mid_re = [re[:, c] * turns[c][0] + im[:, c] * turns[c][1] for c in range(2)]
        mid_im = [im[:, c] * turns[c][0] - re[:, c] * turns[c][1] for c in range(2)]
        mid_re, mid_im = (
            jnp.stack(v, axis=1).reshape(128, HALF).astype(BF) for v in swap_first(mid_re, mid_im)
        )
        total = dot(mid_re, t_ref[:, :HALF], ((1,), (1,)))
        total = total + dot(mid_im, t_ref[:, HALF:], ((1,), (1,)))
        ref[...] = total.astype(BF)


def kernel_g(idx_ref, g_ref, far_ref, head_ref, own_ref, mirror_ref, flip_ref, out_ref, rows):
    place = idx_ref[0]
    kind = jnp.where(
        place == 0, 0, jnp.where(place == 32, 3, jnp.where(place < 32, 1, 2))
    )
    rows[:, :48, :] = g_ref[...]
    rows[:, 48:80, :] = far_ref[...]
    rows[:, 80:96, :] = jnp.zeros((2, 16, N), BF)
    rows[:, 96:, :] = jnp.zeros((2, 16, N), BF)
    rows[:, 96:104, :] = head_ref[...]
    row = lax.broadcasted_iota(jnp.int32, (64, N), 0)
    shifted = ((row & 7) == 0) & (place == 0)
    for ri in range(2):
        near = dot(own_ref[kind], rows[ri])
        far = dot(mirror_ref[kind], rows[ri]).astype(BF)
        far = dot(far, flip_ref[...])
        far = jnp.where(shifted, pltpu.roll(far, 1, 1), far)
        out_ref[ri] = (near + far if ri == 0 else near - far).astype(BF)


def body(signal, cotangent, filter_spec):
    shape = signal.shape
    place = lax.axis_index("seq").astype(jnp.int32).reshape(1)
    table = jnp.asarray(first_table())
    cos_t, sin_t = (jnp.asarray(t) for t in unit_tables())
    flip = jnp.asarray(np.eye(N, dtype=np.float32)[::-1].astype(BF))
    tail, head = (jnp.asarray(t) for t in payload_selectors())
    f_own, f_mirror = (jnp.asarray(t) for t in filter_selectors())
    g_own, g_mirror = (jnp.asarray(t) for t in grad_selectors())
    gather = jnp.asarray(gather_tables())
    opposite = [(d, SEQ - 1 - d) for d in range(SEQ)]
    down = [(d, d // 32 * 32 + (d - 1) % 32) for d in range(SEQ)]
    up = [(b, a) for a, b in down]
    filt = filter_spec.reshape(2, 64, N)
    sent, tails, heads = pl.pallas_call(
        kernel_a,
        in_specs=[SMEM] + [VMEM] * 6,
        out_specs=[VMEM] * 3,
        out_shape=[
            jax.ShapeDtypeStruct((N, HALF), BF),
            jax.ShapeDtypeStruct((2, 32, N), BF),
            jax.ShapeDtypeStruct((2, 8, N), BF),
        ],
        scratch_shapes=[
            pltpu.VMEM((2, 256, 128), F32),
            pltpu.VMEM((2, 256, 128), F32),
            pltpu.VMEM((2, N, 128), F32),
        ],
    )(place, signal.reshape(128, N), cotangent.reshape(128, N), table, filt, tail, head)
    got = lax.all_to_all(sent.reshape(SEQ, ROWS, HALF), "seq", 0, 0, tiled=True)
    tails = lax.ppermute(tails, "seq", opposite)
    heads = lax.ppermute(heads, "seq", down)
    spread = pl.pallas_call(
        kernel_f,
        in_specs=[SMEM] + [VMEM] * 6,
        out_specs=VMEM,
        out_shape=jax.ShapeDtypeStruct((N, N), F32),
        scratch_shapes=[pltpu.VMEM((2, 112, N), BF)],
        compiler_params=PARAMS,
        cost_estimate=pl.CostEstimate(flops=400000000, bytes_accessed=2000000, transcendentals=0),
    )(place, filt, tails, heads, f_own, f_mirror, flip)
    back, grad = pl.pallas_call(
        kernel_b,
        in_specs=[SMEM] + [VMEM] * 5,
        out_specs=[VMEM, VMEM],
        out_shape=[
            jax.ShapeDtypeStruct((N, HALF), BF),
            jax.ShapeDtypeStruct((2, 48, N), BF),
        ],
        scratch_shapes=[pltpu.VMEM((N, HALF), BF)],
        compiler_params=PARAMS,
    )(place, got.reshape(N, HALF), cos_t, sin_t, spread, gather)
    far = lax.ppermute(grad[:, :32], "seq", opposite)
    slot = jnp.where(place[0] == LAST, grad[:, 32:40], grad[:, :8])
    slot = lax.ppermute(slot, "seq", up)
    mid = lax.all_to_all(back.reshape(SEQ, ROWS, HALF), "seq", 0, 0, tiled=True)
    grad = pl.pallas_call(
        kernel_g,
        in_specs=[SMEM] + [VMEM] * 6,
        out_specs=VMEM,
        out_shape=jax.ShapeDtypeStruct((2, 64, N), BF),
        scratch_shapes=[pltpu.VMEM((2, 112, N), BF)],
        compiler_params=PARAMS,
        cost_estimate=pl.CostEstimate(flops=100000000, bytes_accessed=1000000, transcendentals=0),
    )(place, grad, far, slot, g_own, g_mirror, flip)
    for bit in (2, 4, 1):
        other = lax.ppermute(grad, "dp", [(d, d ^ bit) for d in range(8)])
        grad = (grad.astype(F32) + other.astype(F32)).astype(BF)
    output, grad_signal = pl.pallas_call(
        kernel_c,
        in_specs=[SMEM, VMEM, VMEM],
        out_specs=[VMEM, VMEM],
        out_shape=[jax.ShapeDtypeStruct((128, N), BF)] * 2,
        scratch_shapes=[
            pltpu.VMEM((2, N, 128), F32),
            pltpu.VMEM((2, 256, 128), F32),
            pltpu.VMEM((2, 256, 128), F32),
        ],
        compiler_params=PARAMS,
        cost_estimate=pl.CostEstimate(flops=400000000, bytes_accessed=2000000, transcendentals=0),
    )(place, mid.reshape(N, HALF), table)
    return output.reshape(shape), grad_signal.reshape(shape), grad.reshape(2, 8, 8, N)


def solution(mesh):
    placed = (P(None, "dp", "seq", None), P(None, "dp", "seq", None), P(None, None, "seq", None))
    return jax.shard_map(body, mesh=mesh, in_specs=placed, out_specs=placed, check_vma=False)
```
